32 devices in a mesh: gx: 4 (over y, x), gy: 8 (over z, core).
Axes of the slice: x: 2, y: 2, z: 4, core: 2. Of those that a mesh axis runs over, the one named last changes fastest.
Arguments:
- right_side: float32 [8, 3, 64, 1024], P(None, None, 'gx', 'gy'), may hold values from -50 to 50
- first_guess: float32 [8, 3, 64, 1024], P(None, None, 'gx', 'gy'), may hold values from -3 to 3
- diag_block: bfloat16 [8, 3, 3, 64, 1024], P(None, None, None, 'gx', 'gy'), may hold values from -2.41 to 12
- mobility: bfloat16 [8, 3, 3, 64, 1024], P(None, None, None, 'gx', 'gy'), may hold values from -1 to 1.21
- face_trans: bfloat16 [6, 8, 64, 1024], P(None, None, 'gx', 'gy'), may hold values from 0.19921875 to 1
- column_inverse: bfloat16 [4, 6, 6, 64, 1024], P(None, None, None, 'gx', 'gy'), may hold values from -0.061 to 0.201
- perf_cell: int32 [32, 32, 40], P(('gx', 'gy')), may hold values from 0 to 16383, as said below
- perf_slot: int32 [32, 32, 40], P(('gx', 'gy')), may hold values from 0 to 1024, as said below
- well_in: float32 [3, 32768], P(None, ('gx', 'gy')), may hold values from -4 to 4
- well_out: float32 [3, 32768], P(None, ('gx', 'gy')), may hold values from -4 to 4
- well_inverse: float32 [256, 128, 128], P(('gx', 'gy')), may hold values from -1 to 1
Outputs:
- solution: float32 [8, 3, 64, 1024], P(None, None, 'gx', 'gy')
- residual: float32 [8, 3, 64, 1024], P(None, None, 'gx', 'gy')
The draws below stay inside these ranges and needn't reach their ends.
Inputs may be any that keep to these rules, and one draw needn't show every extreme that they name: `perf_cell`: entry [s, d, q] is a local cell number of device s's tile, the cell of slot q from device s to owner d; the slot's segment is perf_slot[d, s, q]; slots that perf_slot marks empty carry an arbitrary cell. `perf_slot`: entry [d, s, q] is w * 128 + g when slot q from device s carries segment g of owner d's local well w, and 1024 when the slot is empty. Each segment of an owner appears at most once; the segments of a well that appear are 0 to n - 1 for its padded count n of 1 to 128. Every pair (d, s) has at most 40 live slots and some pair has exactly 40; in every draw some owner has all 1024 segments live.
All inputs are finite; a program needn't handle non-finite values.
Results may differ from the reference program's by a relative error of at most 0.0003.
Values sent between devices are 32-bit elements; how exact they have to be, the bound alone decides.
No kernel may reach another device: no remote copies, remote signals or barrier semaphores. Data moves between devices by JAX's collectives and lax.ppermute only.
A program may use at most 128 MiB of HBM per device.

```python
import math
import jax
import jax.numpy as jnp
from jax import lax

CX = 16
CY = 128
NZ = 8
W_DEV = 8
SEG = 128
ITERS = 2
NX = 64
NY = 1024
WELLS = 256
CAP = 40
N_GY = 8
DEVICES = 32


def block_matrix(key, full_shape, row_dim, col_dim, low_diag, high_diag, off_scale):
    subkeys = jax.random.split(key, 2)
    row_pos = lax.broadcasted_iota(jnp.int32, full_shape, row_dim)
    col_pos = lax.broadcasted_iota(jnp.int32, full_shape, col_dim)
    leading = jnp.exp(jax.random.uniform(subkeys[0], full_shape, jnp.float32, math.log(low_diag), math.log(high_diag)))
    spread = jnp.clip(jax.random.normal(subkeys[1], full_shape, jnp.float32), -3.0, 3.0) * off_scale
    return jnp.where(row_pos == col_pos, leading, spread)


def draw_right_side(key, part):
    subkeys = jax.random.split(key, 2)
    full_shape = (NZ, 3, NX, NY)
    second_pos = lax.broadcasted_iota(jnp.float32, full_shape, 3) / max(NY - 1, 1)
    cell_scale = jnp.exp(jax.random.uniform(subkeys[1], full_shape, jnp.float32, math.log(0.3), math.log(3.0)))
    ramp_second = 1.0 + 2.0 * second_pos
    rough = jnp.clip(jax.random.normal(subkeys[0], full_shape, jnp.float32), -4.0, 4.0)
    return rough * cell_scale * ramp_second


def draw_diag_block(key, part):
    return block_matrix(key, (NZ, 3, 3, NX, NY), 1, 2, 6.0, 12.0, 0.8).astype(jnp.bfloat16)


def draw_mobility(key, part):
    return block_matrix(key, (NZ, 3, 3, NX, NY), 1, 2, 0.5, 1.2, 0.25).astype(jnp.bfloat16)


def draw_column_inverse(key, part):
    return block_matrix(key, (NZ // 2, 6, 6, NX, NY), 1, 2, 0.08, 0.2, 0.02).astype(jnp.bfloat16)


def draw_well_inverse(key, part):
    return block_matrix(key, (WELLS, SEG, SEG), 1, 2, 0.3, 1.0, 0.3 / math.sqrt(SEG))


def perforation_tables(key):
    subkeys = jax.random.split(jax.random.fold_in(key, 17), 6)
    slot_total = DEVICES * CAP
    longest = jax.random.randint(subkeys[0], (DEVICES, 1), max(SEG // 4, 1), SEG + 1)
    shortest = jnp.maximum(longest // 2, 1)
    counts = jax.random.randint(subkeys[1], (DEVICES, W_DEV), shortest, longest + 1)
    heavy_owner = jax.random.randint(subkeys[2], (), 0, DEVICES)
    owners = jnp.arange(DEVICES, dtype=jnp.int32)[:, None]
    counts = jnp.where(owners == heavy_owner, SEG, counts).astype(jnp.int32)
    seg_ends = jnp.cumsum(counts, axis=1).astype(jnp.int32)
    starts = seg_ends - counts
    live_total = seg_ends[:, -1:]
    forced = jax.random.randint(subkeys[3], (DEVICES, 1), 0, DEVICES)
    position = jnp.arange(slot_total, dtype=jnp.int32)[None, :]
    scores = jax.random.randint(subkeys[4], (DEVICES, slot_total), 1, 1024) * slot_total + position
    scores = jnp.where(position // CAP == forced, position, scores)
    sorted_order = jnp.argsort(scores, axis=1, stable=True)
    slot_rank = jnp.argsort(sorted_order, axis=1, stable=True).astype(jnp.int32)
    well_of = jnp.sum((seg_ends[:, None, :] <= slot_rank[:, :, None]).astype(jnp.int32), axis=2)
    well_of = jnp.minimum(well_of, W_DEV - 1)
    segment = slot_rank - jnp.take_along_axis(starts, well_of, axis=1)
    target = jnp.where(slot_rank < live_total, well_of * SEG + segment, W_DEV * SEG).astype(jnp.int32)
    cell_ids = jax.random.randint(subkeys[5], (DEVICES, slot_total), 0, NZ * CX * CY).astype(jnp.int32)
    return (target.reshape(DEVICES, DEVICES, CAP), cell_ids.reshape(DEVICES, DEVICES, CAP))


def draw_perf_cell(key, part):
    target, cell_ids = perforation_tables(key)
    return jnp.transpose(cell_ids, (1, 0, 2))


def draw_perf_slot(key, part):
    target, cell_ids = perforation_tables(key)
    return target


def level_of(own_key, shape, cuts, low, top_value):
    level = 1.0
    for dim, shards_of in cuts:
        heights = jax.random.uniform(jax.random.fold_in(jax.random.fold_in(own_key, 6), dim), (shards_of,), jnp.float32, low / len(cuts), top_value / len(cuts))
        level = level * jnp.repeat(jnp.exp(heights), shape[dim] // shards_of).reshape((-1,) + (1,) * (len(shape) - 1 - dim))
    return level


def normal_values(stream_key, dims, scale, reach, cuts=(), held_as=jnp.bfloat16):
    level = level_of(stream_key, dims, cuts, -0.22, 0.18) if cuts else 1.0
    entries = jax.random.normal(stream_key, dims, jnp.float32) * scale * level
    return jnp.minimum(jnp.maximum(entries, -reach), reach).astype(held_as)


def setup_inputs(seed: int = 0) -> dict:
    key_list = jax.random.split(jax.random.key(seed), 12)
    right_side = draw_right_side(jax.random.fold_in(key_list[11], 71), 0)
    first_guess = normal_values(key_list[1], (NZ, 3, NX, NY), 0.5, 3.0, ((2, 4), (3, 8)), jnp.float32)
    diag_block = draw_diag_block(jax.random.fold_in(key_list[11], 71), 0)
    mobility = draw_mobility(jax.random.fold_in(key_list[11], 71), 0)
    face_trans = jnp.clip(0.19921875 + 0.80078125 * jax.random.uniform(key_list[4], (6, NZ, NX, NY), jnp.float32) ** level_of(key_list[4], (6, NZ, NX, NY), ((2, 4), (3, 8)), -0.2, 0.2), 0.19921875, 1.0).astype(jnp.bfloat16)
    column_inverse = draw_column_inverse(jax.random.fold_in(key_list[11], 71), 0)
    perf_cell = draw_perf_cell(jax.random.fold_in(key_list[11], 71), 0)
    perf_slot = draw_perf_slot(jax.random.fold_in(key_list[11], 71), 0)
    well_in = normal_values(key_list[8], (3, WELLS * SEG), 0.7, 4.0, ((1, 32),), jnp.float32)
    well_out = normal_values(key_list[9], (3, WELLS * SEG), 0.7, 4.0, ((1, 32),), jnp.float32)
    well_inverse = draw_well_inverse(jax.random.fold_in(key_list[11], 71), 0)
    return {"right_side": right_side, "first_guess": first_guess, "diag_block": diag_block, "mobility": mobility, "face_trans": face_trans, "column_inverse": column_inverse, "perf_cell": perf_cell, "perf_slot": perf_slot, "well_in": well_in, "well_out": well_out, "well_inverse": well_inverse}


def couple(mixing, vector):
    summed = mixing[:, :, 0].astype(jnp.float32) * vector[:, 0:1]
    summed = summed + mixing[:, :, 1].astype(jnp.float32) * vector[:, 1:2]
    summed = summed + mixing[:, :, 2].astype(jnp.float32) * vector[:, 2:3]
    return summed


def stencil(vector, extended, diag_block, face_trans):
    factor = face_trans.astype(jnp.float32)[:, :, None]
    interior = extended[:, :, 1:-1, 1:-1]
    zero_layer = jnp.zeros_like(interior[:1])
    under_layer = jnp.concatenate([zero_layer, interior[:-1]], axis=0)
    over_layer = jnp.concatenate([interior[1:], zero_layer], axis=0)
    beside = factor[0] * extended[:, :, :-2, 1:-1]
    beside = beside + factor[1] * extended[:, :, 2:, 1:-1]
    beside = beside + factor[2] * extended[:, :, 1:-1, :-2]
    beside = beside + factor[3] * extended[:, :, 1:-1, 2:]
    beside = beside + factor[4] * under_layer
    beside = beside + factor[5] * over_layer
    return couple(diag_block, vector) - beside


def precondition(vector, column_inverse):
    layers, comps, tile_rows, tile_cols = vector.shape
    paired = vector.reshape(layers // 2, 6, tile_rows, tile_cols)
    result = column_inverse[:, :, 0].astype(jnp.float32) * paired[:, 0:1]
    for member in range(1, 6):
        result = result + column_inverse[:, :, member].astype(jnp.float32) * paired[:, member:member + 1]
    return result.reshape(vector.shape)


def well_term(vector, perf_cell, perf_slot, well_in, well_out, well_inverse):
    source = jnp.arange(DEVICES, dtype=jnp.int32)[:, None, None]
    owner_id = jnp.arange(DEVICES, dtype=jnp.int32)[None, :, None]
    layer_idx = perf_cell // (CX * CY)
    in_tile = perf_cell % (CX * CY)
    first_idx = (source // N_GY) * CX + in_tile // CY
    second_idx = (source % N_GY) * CY + in_tile % CY
    values = vector[layer_idx, :, first_idx, second_idx]
    local_slot = jnp.transpose(perf_slot, (1, 0, 2))
    per_owner = W_DEV * SEG
    target = jnp.where(local_slot < per_owner, owner_id * per_owner + local_slot, WELLS * SEG).astype(jnp.int32)
    pad_in = jnp.concatenate([well_in, jnp.zeros((3, 1), jnp.float32)], axis=1)
    pad_out = jnp.concatenate([well_out, jnp.zeros((3, 1), jnp.float32)], axis=1)
    rate = pad_in[0][target] * values[..., 0] + pad_in[1][target] * values[..., 1] + pad_in[2][target] * values[..., 2]
    totals = jnp.zeros((WELLS * SEG + 1,), jnp.float32).at[target].add(rate)
    seg_rate = jnp.einsum("wgh,wh->wg", well_inverse.astype(jnp.float32), totals[:WELLS * SEG].reshape(WELLS, SEG), precision=lax.Precision.HIGHEST)
    padded = jnp.concatenate([seg_rate.reshape(-1), jnp.zeros((1,), jnp.float32)])
    back = padded[target]
    terms = jnp.stack([pad_out[0][target] * back, pad_out[1][target] * back, pad_out[2][target] * back], axis=-1)
    return jnp.zeros_like(vector).at[layer_idx, :, first_idx, second_idx].add(terms)


def reference(right_side, first_guess, diag_block, mobility, face_trans, column_inverse, perf_cell, perf_slot, well_in, well_out, well_inverse):
    def apply_operator(vector):
        flux = couple(mobility, vector)
        extended = jnp.pad(flux, ((0, 0), (0, 0), (1, 1), (1, 1)))
        return stencil(vector, extended, diag_block, face_trans) - well_term(vector, perf_cell, perf_slot, well_in, well_out, well_inverse)

    iterate = first_guess
    residual = right_side - apply_operator(iterate)
    shadow = residual
    inner_now = jnp.sum(shadow * residual)
    search = residual
    for iteration in range(ITERS):
        search_hat = precondition(search, column_inverse)
        applied = apply_operator(search_hat)
        projected = jnp.sum(shadow * applied)
        step_size = inner_now / projected
        halfway = residual - step_size * applied
        halfway_hat = precondition(halfway, column_inverse)
        response = apply_operator(halfway_hat)
        smoothing = jnp.sum(response * halfway) / jnp.sum(response * response)
        iterate = iterate + step_size * search_hat + smoothing * halfway_hat
        residual = halfway - smoothing * response
        if iteration + 1 < ITERS:
            inner_next = jnp.sum(shadow * residual)
            momentum = (inner_next / inner_now) * (step_size / smoothing)
            search = residual + momentum * (search - smoothing * applied)
            inner_now = inner_next
    return iterate, right_side - apply_operator(iterate)
```

```python
import functools

import jax
import jax.numpy as jnp
from jax import lax
from jax.experimental import pallas as pl
from jax.experimental.pallas import tpu as pltpu
from jax.sharding import PartitionSpec as P

ITERS = 2
AXES = ("gx", "gy")
LANES = 128
SUBS = 8
F32 = jnp.float32
BF16 = jnp.bfloat16
SCOPED = 16 * 1024 * 1024


class Geometry:
    def __init__(self, vector_shape, table_shape, inverse_shape, n_gy):
        self.layers, self.comps, self.rows, self.cols = vector_shape
        self.devices, self.cap = table_shape
        self.wells, self.segs = inverse_shape[:2]
        self.n_gy = n_gy
        self.tile_rows = self.layers * self.rows
        self.faces = self.layers * self.comps
        self.per = LANES // self.cap
        self.groups = -(-self.devices // self.per)
        self.groups_pad = -(-self.groups // SUBS) * SUBS
        self.vector = (self.layers, self.comps, self.rows, self.cols)
        self.padded = (self.faces, self.rows + 2 * SUBS, self.cols)
        assert self.cols == LANES and self.segs == LANES and self.rows == 2 * SUBS
        assert self.faces + SUBS <= self.devices and 2 * self.faces <= LANES
        assert 3 * self.cap <= LANES

    def pieces(self):
        for k in range(self.per):
            low = k * self.groups
            count = min(self.groups, self.devices - low)
            if count > 0:
                yield k, low, count


def call(body, outs, args, scratch=()):
    spec = pl.BlockSpec(memory_space=pltpu.VMEM)
    held = [pltpu.with_memory_space_constraint(a, pltpu.VMEM) for a in args]
    return pl.pallas_call(
        body,
        out_shape=tuple(pltpu.VMEM(shape, dtype) for shape, dtype in outs),
        in_specs=[spec] * len(held),
        out_specs=(spec,) * len(outs),
        scratch_shapes=list(scratch),
        compiler_params=pltpu.CompilerParams(vmem_limit_bytes=SCOPED),
    )(*held)


def iota(shape, dim):
    return lax.broadcasted_iota(jnp.int32, shape, dim)


def take_lanes(table, index):
    return jnp.take_along_axis(table, index, axis=1, mode="promise_in_bounds")


def spread(row, shape):
    return jnp.broadcast_to(row, shape)


def total(block):
    return jnp.sum(jnp.sum(block, axis=0, keepdims=True), axis=1, keepdims=True)


def pack_slots(geo, block_ref, lane, packed_ref):
    packed_ref[...] = jnp.zeros_like(packed_ref)
    start = lane // LANES * LANES
    for k, low, count in geo.pieces():
        part = block_ref[low : low + count, start : start + LANES]
        shift = (k * geo.cap - lane) % LANES
        part = pltpu.roll(part, shift, 1) if shift else part
        at = iota(part.shape, 1)
        mine = (at >= k * geo.cap) & (at < (k + 1) * geo.cap)
        packed_ref[0:count, :] = jnp.where(mine, part, packed_ref[0:count, :])


def unpack_slots(geo, packed, lane, block_ref):
    for k, low, count in geo.pieces():
        shift = (lane - k * geo.cap) % LANES
        part = pltpu.roll(packed, shift, 1) if shift else packed
        part = part[0:count]
        at = iota(part.shape, 1)
        mine = (at >= lane) & (at < lane + geo.cap)
        block_ref[low : low + count, 0:LANES] = jnp.where(
            mine, part, block_ref[low : low + count, 0:LANES]
        )


def setup_body(geo, cell_ref, slot_ref, inverse_ref, rowp, lanep, row_hot, lane_hot, hi, lo, inv_dev, inv_pos, turned, wide, packed):
    shape = (geo.devices, LANES)
    wide[...] = jnp.zeros_like(wide)
    wide[:, 0 : geo.cap] = cell_ref[...] + 1
    pack_slots(geo, wide, 0, packed)
    cells = packed[...] - 1
    row = cells >> 7
    lane = cells & (LANES - 1)
    rowp[...] = row
    lanep[...] = lane
    for g in range(geo.groups):
        here = slice(g * LANES, (g + 1) * LANES)
        rows = spread(row[g : g + 1], (geo.tile_rows, LANES))
        row_hot[:, here] = jnp.where(rows == iota(rows.shape, 0), 1.0, 0.0).astype(BF16)
        lanes = spread(lane[g : g + 1], (LANES, LANES))
        lane_hot[:, here] = jnp.where(lanes == iota(lanes.shape, 0), 1.0, 0.0).astype(BF16)
    wide[:, 0 : geo.cap] = slot_ref[...] + 1
    slots = wide[...] - 1
    hi[...] = slots >> 7
    lo[...] = slots & (LANES - 1)
    pack_slots(geo, wide, 0, packed)
    slots = packed[...] - 1
    slot_hi = slots >> 7
    slot_lo = slots & (LANES - 1)
    at = iota((geo.wells, LANES), 1)
    piece = lax.div(at, geo.cap)
    position = (lax.rem(at, geo.cap) + 1).astype(F32)
    found = jnp.zeros((2 * geo.wells, LANES), F32)
    for g in range(geo.groups):
        well = spread(slot_hi[g : g + 1], (geo.wells, LANES)) == iota((geo.wells, LANES), 0)
        device = (piece * geo.groups + (g + 1)).astype(F32)
        marks = jnp.concatenate([jnp.where(well, device, 0.0), jnp.where(well, position, 0.0)], axis=0)
        segs = spread(slot_lo[g : g + 1], (LANES, LANES))
        hot = jnp.where(segs == iota(segs.shape, 0), 1.0, 0.0).astype(BF16)
        found += lax.dot_general(marks.astype(BF16), hot, (((1,), (1,)), ((), ())), preferred_element_type=F32)
    inv_dev[...] = found[: geo.wells].astype(jnp.int32) - 1
    inv_pos[...] = jnp.maximum(found[geo.wells :].astype(jnp.int32) - 1, 0)
    for w in range(geo.wells):
        turned[w] = inverse_ref[w].T


def write_faces(geo, flux, send):
    one, two, three = LANES, 2 * LANES, 3 * LANES
    if geo.devices > geo.faces + SUBS:
        send[geo.faces + SUBS :, one:three] = jnp.zeros((geo.devices - geo.faces - SUBS, 2 * LANES), F32)
    at = iota((geo.rows, LANES), 1)
    edges = jnp.zeros((geo.rows, LANES), F32)
    for j in range(geo.faces):
        block = flux[j, SUBS : SUBS + geo.rows, :]
        send[j : j + 1, one:two] = flux[j, SUBS : SUBS + 1, :]
        send[j : j + 1, two:three] = flux[j, SUBS + geo.rows - 1 : SUBS + geo.rows, :]
        turned = pltpu.roll(block, 2 * j + 1, 1)
        edges = jnp.where((at >> 1) == j, turned, edges)
    send[geo.faces : geo.faces + SUBS, one:two] = edges[:SUBS]
    send[geo.faces : geo.faces + SUBS, two:three] = edges[SUBS:]


def write_flux(geo, mobility, vector, flux):
    for z in range(geo.layers):
        v = [vector[z, b] for b in range(3)]
        for a in range(3):
            block = mobility[z, a, 0].astype(F32) * v[0]
            block += mobility[z, a, 1].astype(F32) * v[1]
            block += mobility[z, a, 2].astype(F32) * v[2]
            flux[3 * z + a, SUBS : SUBS + geo.rows, :] = block


def gather_cells(geo, vector, rowp, lanep, finish):
    shape = (SUBS, LANES)
    for g in range(geo.groups):
        lane = spread(lanep[g : g + 1, :], shape)
        row = spread(rowp[g : g + 1, :], shape) - iota(shape, 0)
        kept = [jnp.zeros(shape, F32) for _ in range(3)]
        for z in range(geo.layers):
            for h in range(geo.rows // SUBS):
                mine = row == z * geo.rows + h * SUBS
                for c in range(3):
                    found = take_lanes(vector[z, c, h * SUBS : (h + 1) * SUBS, :], lane)
                    kept[c] = jnp.where(mine, found, kept[c])
        finish(g, kept)


def precondition(geo, inverse, source, target):
    for h in range(geo.layers // 2):
        v = [source[2 * h + f // 3, f % 3] for f in range(6)]
        for e in range(6):
            block = inverse[h, e, 0].astype(F32) * v[0]
            for f in range(1, 6):
                block += inverse[h, e, f].astype(F32) * v[f]
            target[2 * h + e // 3, e % 3] = block


def first_body(geo, guess, mobility, rowp, lanep, flux, send, packed):
    write_flux(geo, mobility, guess, flux)
    write_faces(geo, flux, send)
    send[:, 0:LANES] = jnp.zeros((geo.devices, LANES), F32)
    packed[...] = jnp.zeros_like(packed)

    def finish(g, kept):
        for c in range(3):
            packed[c, g : g + 1, :] = jnp.sum(kept[c], axis=0, keepdims=True)

    gather_cells(geo, guess, rowp, lanep, finish)
    for c in range(3):
        unpack_slots(geo, packed[c], c * geo.cap, send)


def relay(geo, me, came, back):
    shape = (geo.devices, LANES)
    at = iota(shape, 0)
    even = (iota(shape, 1) & 1) == 0
    within = lax.rem(at, geo.n_gy)
    faces = me[0:1, :] < geo.faces
    up, down, count = geo.n_gy, geo.devices - geo.n_gy, geo.devices
    one = came[:, LANES : 2 * LANES]
    two = came[:, 2 * LANES : 3 * LANES]
    after = jnp.where(at < down, pltpu.roll(one, down, 0), 0.0)
    before = jnp.where(at >= up, pltpu.roll(two, up, 0), 0.0)

    def beside(block):
        low = jnp.where(within > 0, pltpu.roll(block, 1, 0), 0.0)
        high = jnp.where(within < geo.n_gy - 1, pltpu.roll(block, count - 1, 0), 0.0)
        return jnp.where(even, low, high)

    faces = spread(faces, shape)
    back[:, LANES : 2 * LANES] = jnp.where(faces, after, beside(one))
    back[:, 2 * LANES : 3 * LANES] = jnp.where(faces, before, beside(two))


def at_segments(geo, came, inv_dev, inv_pos, offset):
    shape = (geo.wells, LANES)
    device = inv_dev[...]
    position = inv_pos[...] + offset
    kept = jnp.zeros(shape, F32)
    for s in range(geo.devices):
        found = take_lanes(spread(came[s : s + 1, 0:LANES], shape), position)
        kept = jnp.where(device == s, found, kept)
    return kept


def at_slots(geo, rows, hi, lo):
    shape = (geo.devices, LANES)
    kept = jnp.zeros(shape, F32)
    for w in range(geo.wells):
        found = take_lanes(spread(rows[w], shape), lo)
        kept = jnp.where(hi == w, found, kept)
    return kept


def solve_segments(geo, rate, turned):
    rate_t = rate.T
    rows = []
    for w in range(geo.wells):
        rows.append(jnp.sum(turned[w] * rate_t[:, w : w + 1], axis=0, keepdims=True))
    return rows


def owner_first_body(geo, came, me, inv_dev, inv_pos, hi_ref, lo_ref, turned, well_in, well_out, back):
    shape = (geo.wells, LANES)
    hi, lo = hi_ref[...], lo_ref[...]
    rate = jnp.zeros(shape, F32)
    rows_in = [[well_in[c : c + 1, w * LANES : (w + 1) * LANES] for w in range(geo.wells)] for c in range(3)]
    rows_out = [[well_out[c : c + 1, w * LANES : (w + 1) * LANES] for w in range(geo.wells)] for c in range(3)]
    for c in range(3):
        rate += jnp.concatenate(rows_in[c], axis=0) * at_segments(geo, came, inv_dev, inv_pos, c * geo.cap)
    back[:, 0:LANES] = at_slots(geo, solve_segments(geo, rate, turned), hi, lo)
    relay(geo, me, came, back)
    for place, rows in ((3, rows_in), (4, rows_out)):
        block = jnp.zeros((geo.devices, LANES), F32)
        for c in range(3):
            part = at_slots(geo, rows[c], hi, lo)
            block += pltpu.roll(part, c * geo.cap, 1) if c else part
        back[:, place * LANES : (place + 1) * LANES] = block


def owner_body(geo, came, me, inv_dev, inv_pos, hi_ref, lo_ref, turned, back, sums):
    rate = at_segments(geo, came, inv_dev, inv_pos, 0)
    back[:, 0:LANES] = at_slots(geo, solve_segments(geo, rate, turned), hi_ref[...], lo_ref[...])
    relay(geo, me, came, back)
    sums[...] = spread(jnp.sum(came[:, 0:LANES], axis=0, keepdims=True), sums.shape)


def scatter_terms(geo, came, coeff_out, row_hot, lane_hot, packed, spots):
    pack_slots(geo, came, 0, packed)
    width = geo.groups * LANES
    sum_of = None
    parts = []
    for c in range(3):
        value = coeff_out[c] * packed[...]
        high = value.astype(BF16)
        rest = value - high.astype(F32)
        middle = rest.astype(BF16)
        low = (rest - middle.astype(F32)).astype(BF16)
        parts.append((high, middle, low))
    result = None
    for g in range(geo.groups):
        here = slice(g * LANES, (g + 1) * LANES)
        hot = row_hot[:, here]
        left = jnp.concatenate(
            [hot * spread(parts[c][k][g : g + 1], hot.shape) for c in range(3) for k in range(3)], axis=0
        )
        piece = lax.dot_general(left, lane_hot[:, here], (((1,), (1,)), ((), ())), preferred_element_type=F32)
        result = piece if result is None else result + piece
    n = geo.tile_rows
    for c in range(3):
        base = 3 * c * n
        spots[c * n : (c + 1) * n, :] = (
            result[base : base + n] + result[base + n : base + 2 * n] + result[base + 2 * n : base + 3 * n]
        )


def apply_operator(geo, came, vector, flux, diag, face, spots, store):
    shape = (geo.rows, LANES)
    at_row, at_lane = iota(shape, 0), iota(shape, 1)
    one, two, three = LANES, 2 * LANES, 3 * LANES
    edges = jnp.concatenate(
        [came[geo.faces : geo.faces + SUBS, one:two], came[geo.faces : geo.faces + SUBS, two:three]], axis=0
    )
    inside = slice(SUBS, SUBS + geo.rows)
    for z in range(geo.layers):
        f = [face[n, z].astype(F32) for n in range(6)]
        v = [vector[z, b] for b in range(3)]
        for a in range(3):
            j = 3 * z + a
            block = flux[j, inside, :]
            under = jnp.where(at_row == 0, spread(came[j : j + 1, two:three], shape), flux[j, SUBS - 1 : SUBS - 1 + geo.rows, :])
            over = jnp.where(at_row == geo.rows - 1, spread(came[j : j + 1, one:two], shape), flux[j, SUBS + 1 : SUBS + 1 + geo.rows, :])
            left = jnp.where(at_lane == 0, spread(edges[:, 2 * j : 2 * j + 1], shape), pltpu.roll(block, 1, 1))
            right = jnp.where(at_lane == LANES - 1, spread(edges[:, 2 * j + 1 : 2 * j + 2], shape), pltpu.roll(block, LANES - 1, 1))
            beside = f[0] * under + f[1] * over + f[2] * left + f[3] * right
            if z > 0:
                beside += f[4] * flux[j - 3, inside, :]
            if z + 1 < geo.layers:
                beside += f[5] * flux[j + 3, inside, :]
            own = diag[z, a, 0].astype(F32) * v[0]
            own += diag[z, a, 1].astype(F32) * v[1]
            own += diag[z, a, 2].astype(F32) * v[2]
            base = a * geo.tile_rows + z * geo.rows
            store(z, a, own - beside - spots[base : base + geo.rows, :])


def send_next(geo, source, inverse, mobility, rowp, lanep, coeff_in, dots, ahead, flux, send, packed):
    precondition(geo, inverse, source, ahead)
    write_flux(geo, mobility, ahead, flux)
    write_faces(geo, flux, send)
    at = iota((1, LANES), 1)
    row = jnp.zeros((1, LANES), F32)
    for n, dot in enumerate(dots):
        row = jnp.where(at == geo.cap + n, spread(total(dot), (1, LANES)), row)
    send[:, 0:LANES] = spread(row, (geo.devices, LANES))
    packed[...] = jnp.zeros_like(packed)

    def finish(g, kept):
        rate = kept[0] * spread(coeff_in[0, g : g + 1, :], kept[0].shape)
        rate += kept[1] * spread(coeff_in[1, g : g + 1, :], kept[0].shape)
        rate += kept[2] * spread(coeff_in[2, g : g + 1, :], kept[0].shape)
        packed[g : g + 1, :] = jnp.sum(rate, axis=0, keepdims=True)

    gather_cells(geo, ahead, rowp, lanep, finish)
    unpack_slots(geo, packed[...], 0, send)


def each_tile(geo):
    for z in range(geo.layers):
        for c in range(geo.comps):
            yield z, c


COMMON = 8


def stage_zero_body(geo, came, guess, flux_in, diag, face, row_hot, lane_hot, inverse, mobility, rowp, lanep, right_side,
                    shadow, coeff_in, coeff_out, ahead, flux, send, packed, spots):
    for c in range(3):
        pack_slots(geo, came, 3 * LANES + c * geo.cap, packed)
        coeff_in[c] = packed[...]
        pack_slots(geo, came, 4 * LANES + c * geo.cap, packed)
        coeff_out[c] = packed[...]
    scatter_terms(geo, came, coeff_out, row_hot, lane_hot, packed, spots)
    dots = [jnp.zeros((geo.rows, LANES), F32)]

    def store(z, c, image):
        value = right_side[z, c] - image
        shadow[z, c] = value
        dots[0] += value * value

    apply_operator(geo, came, guess, flux_in, diag, face, spots, store)
    send_next(geo, shadow, inverse, mobility, rowp, lanep, coeff_in, dots, ahead, flux, send, packed)


def stage_image_body(geo, came, vector, flux_in, diag, face, row_hot, lane_hot, inverse, mobility, rowp, lanep, coeff_in, coeff_out, shadow,
                     image_out, ahead, flux, send, packed, spots):
    scatter_terms(geo, came, coeff_out, row_hot, lane_hot, packed, spots)
    dots = [jnp.zeros((geo.rows, LANES), F32)]

    def store(z, c, image):
        image_out[z, c] = image
        dots[0] += shadow[z, c] * image

    apply_operator(geo, came, vector, flux_in, diag, face, spots, store)
    send_next(geo, image_out, inverse, mobility, rowp, lanep, coeff_in, dots, ahead, flux, send, packed)


def stage_half_body(geo, came, vector, flux_in, diag, face, row_hot, lane_hot, inverse, mobility, rowp, lanep, coeff_in, coeff_out, shadow,
                    step, residual, applied, behind,
                    deeper, half, response, ahead, flux, send, packed, spots):
    scatter_terms(geo, came, coeff_out, row_hot, lane_hot, packed, spots)
    dots = [jnp.zeros((geo.rows, LANES), F32) for _ in range(4)]
    scale = spread(step[0:1, 0:1], (geo.rows, LANES))

    def store(z, c, image):
        deeper[z, c] = image
        s = residual[z, c] - scale * applied[z, c]
        t = behind[z, c] - scale * image
        half[z, c] = s
        response[z, c] = t
        dots[0] += t * s
        dots[1] += t * t
        dots[2] += shadow[z, c] * t
        dots[3] += shadow[z, c] * s

    apply_operator(geo, came, vector, flux_in, diag, face, spots, store)
    send_next(geo, response, inverse, mobility, rowp, lanep, coeff_in, dots, ahead, flux, send, packed)


def stage_next_body(geo, came, vector, flux_in, diag, face, row_hot, lane_hot, inverse, mobility, rowp, lanep, coeff_in, coeff_out, shadow,
                    smoothing, momentum, half, response, applied, deeper,
                    residual_out, behind_out, applied_out, ahead, flux, send, packed, spots):
    scatter_terms(geo, came, coeff_out, row_hot, lane_hot, packed, spots)
    dots = [jnp.zeros((geo.rows, LANES), F32)]
    smooth = spread(smoothing[0:1, 0:1], (geo.rows, LANES))
    keep = spread(momentum[0:1, 0:1], (geo.rows, LANES))

    def store(z, c, image):
        t = response[z, c]
        residual_out[z, c] = half[z, c] - smooth * t
        w = t - smooth * image
        behind_out[z, c] = w
        v = w + keep * (applied[z, c] - smooth * deeper[z, c])
        applied_out[z, c] = v
        dots[0] += shadow[z, c] * v

    apply_operator(geo, came, vector, flux_in, diag, face, spots, store)
    send_next(geo, applied_out, inverse, mobility, rowp, lanep, coeff_in, dots, ahead, flux, send, packed)


def stage_last_body(geo, came, vector, flux_in, diag, face, row_hot, lane_hot, coeff_out, step, residual, applied, behind,
                    half, response, send, packed, spots):
    scatter_terms(geo, came, coeff_out, row_hot, lane_hot, packed, spots)
    dots = [jnp.zeros((geo.rows, LANES), F32) for _ in range(2)]
    scale = spread(step[0:1, 0:1], (geo.rows, LANES))

    def store(z, c, image):
        s = residual[z, c] - scale * applied[z, c]
        t = behind[z, c] - scale * image
        half[z, c] = s
        response[z, c] = t
        dots[0] += t * s
        dots[1] += t * t

    apply_operator(geo, came, vector, flux_in, diag, face, spots, store)
    at = iota((1, LANES), 1)
    row = jnp.where(at == 0, spread(total(dots[0]), (1, LANES)), spread(total(dots[1]), (1, LANES)))
    send[...] = spread(row, send.shape)


def pick(sums, geo, n):
    return sums[:, geo.cap + n : geo.cap + n + 1]


def ratio_body(geo, upper, sums, step):
    step[...] = spread(upper[:, 0:1] / pick(sums, geo, 0), step.shape)


def scalars_body(geo, sums, rho, step, smoothing, momentum, rho_out):
    smooth = pick(sums, geo, 0) / pick(sums, geo, 1)
    rho_next = pick(sums, geo, 3) - smooth * pick(sums, geo, 2)
    smoothing[...] = spread(smooth, smoothing.shape)
    momentum[...] = spread((rho_next / rho[:, 0:1]) * (step[:, 0:1] / smooth), momentum.shape)
    rho_out[...] = spread(rho_next, rho_out.shape)


def rho_body(geo, sums, rho):
    rho[...] = spread(pick(sums, geo, 0), rho.shape)


def update_body(geo, step, smoothing, momentum, iterate, search_hat, applied_hat, residual_hat, response_hat,
                iterate_out, residual_out, search_out):
    shape = (geo.rows, LANES)
    alpha, omega, beta = (spread(x[0:1, 0:1], shape) for x in (step, smoothing, momentum))
    for z, c in each_tile(geo):
        half_hat = residual_hat[z, c] - alpha * applied_hat[z, c]
        iterate_out[z, c] = iterate[z, c] + alpha * search_hat[z, c] + omega * half_hat
        next_hat = half_hat - omega * response_hat[z, c]
        residual_out[z, c] = next_hat
        search_out[z, c] = next_hat + beta * (search_hat[z, c] - omega * applied_hat[z, c])


def ready_body(geo, step, iterate, search_hat, residual_hat, applied_hat, iterate_out, half_out):
    alpha = spread(step[0:1, 0:1], (geo.rows, LANES))
    for z, c in each_tile(geo):
        iterate_out[z, c] = iterate[z, c] + alpha * search_hat[z, c]
        half_out[z, c] = residual_hat[z, c] - alpha * applied_hat[z, c]


def finish_body(geo, came, iterate, half_hat, half, response, solution_out, residual_out):
    sums = jnp.sum(came[...], axis=0, keepdims=True)
    omega = spread(sums[:, 0:1] / sums[:, 1:2], (geo.rows, LANES))
    for z, c in each_tile(geo):
        solution_out[z, c] = iterate[z, c] + omega * half_hat[z, c]
        residual_out[z, c] = half[z, c] - omega * response[z, c]


def exchange(rows):
    return lax.all_to_all(rows, AXES, split_axis=0, concat_axis=0, tiled=True)


def per_device(right_side, guess, diag, mobility, face, inverse, perf_cell, perf_slot, well_in, well_out, well_inverse):
    geo = Geometry(right_side.shape, perf_cell.shape[1:], well_inverse.shape, lax.axis_size("gy"))
    bind = lambda body: functools.partial(body, geo)
    me = jnp.broadcast_to(lax.axis_index(AXES), (SUBS, LANES)).astype(jnp.int32)
    block = (geo.devices, LANES)
    packed_shape = (geo.groups_pad, LANES)
    wide = (geo.devices, 3 * LANES)
    seg_shape = (geo.wells, LANES)
    small = ((SUBS, LANES), F32)
    vec = (geo.vector, F32)
    hot = geo.groups * LANES
    ints = jnp.int32
    rowp, lanep, row_hot, lane_hot, hi, lo, inv_dev, inv_pos, turned = call(
        bind(setup_body),
        [(packed_shape, ints), (packed_shape, ints), ((geo.tile_rows, hot), BF16), ((LANES, hot), BF16), (block, ints), (block, ints),
         (seg_shape, ints), (seg_shape, ints), (well_inverse.shape, F32)],
        [perf_cell[0], perf_slot[0], well_inverse],
        [pltpu.VMEM(block, ints), pltpu.VMEM(packed_shape, ints)],
    )
    owner_tables = [me, inv_dev, inv_pos, hi, lo, turned]
    packed = pltpu.VMEM(packed_shape, F32)
    spots = pltpu.VMEM((3 * geo.tile_rows, LANES), F32)
    coeffs = ((3,) + packed_shape, F32)
    sent = [vec, (geo.padded, F32), (wide, F32)]

    flux, send = call(
        bind(first_body), [(geo.padded, F32), (wide, F32)], [guess, mobility, rowp, lanep], [pltpu.VMEM((3,) + packed_shape, F32)]
    )
    (back,) = call(bind(owner_first_body), [((geo.devices, 5 * LANES), F32)], [exchange(send)] + owner_tables + [well_in, well_out])
    shadow, coeff_in, coeff_out, ahead, flux, send = call(
        bind(stage_zero_body), [vec, coeffs, coeffs] + sent,
        [exchange(back), guess, flux, diag, face, row_hot, lane_hot, inverse, mobility, rowp, lanep, right_side], [packed, spots],
    )
    hats = [diag, face, row_hot, lane_hot, inverse, mobility, rowp, lanep, coeff_in, coeff_out, shadow]

    def owner(send):
        back, sums = call(bind(owner_body), [(wide, F32), small], [exchange(send)] + owner_tables)
        return exchange(back), sums

    came, sums = owner(send)
    (rho,) = call(bind(rho_body), [small], [sums])
    search_hat = residual_hat = ahead
    applied, ahead, flux, send = call(
        bind(stage_image_body), [vec] + sent, [came, ahead, flux] + hats, [packed, spots]
    )
    residual, behind, iterate = shadow, applied, guess
    for iteration in range(ITERS):
        applied_hat = ahead
        came, sums = owner(send)
        (step,) = call(bind(ratio_body), [small], [rho, sums])
        if iteration + 1 == ITERS:
            half, response, send = call(
                bind(stage_last_body), [vec, vec, (block, F32)],
                [came, ahead, flux, diag, face, row_hot, lane_hot, coeff_out, step, residual, applied, behind], [packed, spots],
            )
            break
        deeper, half, response, ahead, flux, send = call(
            bind(stage_half_body), [vec, vec, vec] + sent, [came, ahead, flux] + hats + [step, residual, applied, behind], [packed, spots]
        )
        response_hat = ahead
        came, sums = owner(send)
        smoothing, momentum, rho = call(bind(scalars_body), [small] * 3, [sums, rho, step])
        residual, behind, applied, ahead, flux, send = call(
            bind(stage_next_body), [vec, vec, vec] + sent,
            [came, ahead, flux] + hats + [smoothing, momentum, half, response, applied, deeper], [packed, spots],
        )
        iterate, residual_hat, search_hat = call(
            bind(update_body), [vec] * 3, [step, smoothing, momentum, iterate, search_hat, applied_hat, residual_hat, response_hat]
        )
    iterate, half_hat = call(bind(ready_body), [vec] * 2, [step, iterate, search_hat, residual_hat, applied_hat])
    return call(bind(finish_body), [vec] * 2, [exchange(send), iterate, half_hat, half, response])


def solution(mesh):
    in_specs = (
        P(None, None, "gx", "gy"),
        P(None, None, "gx", "gy"),
        P(None, None, None, "gx", "gy"),
        P(None, None, None, "gx", "gy"),
        P(None, None, "gx", "gy"),
        P(None, None, None, "gx", "gy"),
        P(AXES, None, None),
        P(AXES, None, None),
        P(None, AXES),
        P(None, AXES),
        P(AXES, None, None),
    )
    out_specs = (P(None, None, "gx", "gy"), P(None, None, "gx", "gy"))
    return jax.shard_map(per_device, mesh=mesh, in_specs=in_specs, out_specs=out_specs, check_vma=False)
```

```python
import functools

import jax
import jax.numpy as jnp
from jax import lax
from jax.experimental import pallas as pl
from jax.experimental.pallas import tpu as pltpu
from jax.sharding import PartitionSpec as P

ITERS = 2
AXES = ("gx", "gy")
LANES = 128
SUBS = 8
F32 = jnp.float32
BF16 = jnp.bfloat16
SCOPED = 16 * 1024 * 1024


class Geometry:
    def __init__(self, vector_shape, table_shape, inverse_shape, n_gy):
        self.layers, self.comps, self.rows, self.cols = vector_shape
        self.devices, self.cap = table_shape
        self.wells, self.segs = inverse_shape[:2]
        self.n_gy = n_gy
        self.tile_rows = self.layers * self.rows
        self.half_rows = self.tile_rows // 2
        self.faces = self.layers * self.comps
        self.per = LANES // self.cap
        self.groups = -(-self.devices // self.per)
        self.groups_pad = -(-self.groups // SUBS) * SUBS
        self.slots = self.groups * LANES
        self.vector = (self.layers, self.comps, self.rows, self.cols)
        self.flux = (self.faces * self.rows + 2 * SUBS, self.cols)
        self.tile = (self.rows, LANES)
        assert self.cols == LANES and self.segs == LANES and self.rows == 2 * SUBS
        assert self.faces + SUBS <= self.devices and 2 * self.faces <= LANES
        assert 3 * self.cap <= LANES

    def pieces(self):
        for k in range(self.per):
            low = k * self.groups
            count = min(self.groups, self.devices - low)
            if count > 0:
                yield k, low, count

    def tiles(self):
        for z in range(self.layers):
            for c in range(self.comps):
                yield z, c

    def base(self, j):
        return SUBS + j * self.rows


HELD = pl.BlockSpec(memory_space=pltpu.VMEM)
FAR = pl.BlockSpec(memory_space=pltpu.HBM)


def call(body, outs, args, far=(), scratch=(), out_far=False):
    held = [pltpu.with_memory_space_constraint(a, pltpu.VMEM) for a in args]
    far = [pltpu.with_memory_space_constraint(a, pltpu.HBM) for a in far]
    shapes = [jax.ShapeDtypeStruct(*o) if out_far else pltpu.VMEM(*o) for o in outs]
    return pl.pallas_call(
        body,
        out_shape=tuple(shapes),
        in_specs=[HELD] * len(held) + [FAR] * len(far),
        out_specs=(FAR if out_far else HELD,) * len(outs),
        scratch_shapes=list(scratch),
        compiler_params=pltpu.CompilerParams(vmem_limit_bytes=SCOPED),
    )(*held, *far)


def iota(shape, dim):
    return lax.broadcasted_iota(jnp.int32, shape, dim)


def take_lanes(table, index):
    return jnp.take_along_axis(table, index, axis=1, mode="promise_in_bounds")


def spread(row, shape):
    return jnp.broadcast_to(row, shape)


def total(block):
    return jnp.sum(jnp.sum(block, axis=0, keepdims=True), axis=1, keepdims=True)


def one_hot(index, size):
    rows = spread(index, (size, LANES))
    return jnp.where(rows == iota(rows.shape, 0), 1.0, 0.0).astype(BF16)


def pack_slots(geo, block_ref, lane, packed_ref):
    packed_ref[...] = jnp.zeros_like(packed_ref)
    start = lane // LANES * LANES
    for k, low, count in geo.pieces():
        part = block_ref[low : low + count, start : start + LANES]
        shift = (k * geo.cap - lane) % LANES
        part = pltpu.roll(part, shift, 1) if shift else part
        at = iota(part.shape, 1)
        mine = (at >= k * geo.cap) & (at < (k + 1) * geo.cap)
        packed_ref[0:count, :] = jnp.where(mine, part, packed_ref[0:count, :])


def unpack_slots(geo, packed, lane, block_ref):
    for k, low, count in geo.pieces():
        shift = (lane - k * geo.cap) % LANES
        part = pltpu.roll(packed, shift, 1) if shift else packed
        part = part[0:count]
        at = iota(part.shape, 1)
        mine = (at >= lane) & (at < lane + geo.cap)
        block_ref[low : low + count, 0:LANES] = jnp.where(
            mine, part, block_ref[low : low + count, 0:LANES]
        )


def write_faces(geo, flux, send):
    one, two, three = LANES, 2 * LANES, 3 * LANES
    if geo.devices > geo.faces + SUBS:
        send[geo.faces + SUBS :, one:three] = jnp.zeros((geo.devices - geo.faces - SUBS, 2 * LANES), F32)
    send[0 : geo.faces, one:two] = flux[pl.ds(geo.base(0), geo.faces, stride=geo.rows), :]
    send[0 : geo.faces, two:three] = flux[pl.ds(geo.base(0) + geo.rows - 1, geo.faces, stride=geo.rows), :]
    at = iota(geo.tile, 1) >> 1
    edges = jnp.zeros(geo.tile, F32)
    for j in range(geo.faces):
        turned = pltpu.roll(flux[geo.base(j) : geo.base(j) + geo.rows, :], 2 * j + 1, 1)
        edges = jnp.where(at == j, turned, edges)
    send[geo.faces : geo.faces + SUBS, one:two] = edges[:SUBS]
    send[geo.faces : geo.faces + SUBS, two:three] = edges[SUBS:]


def write_flux(geo, mobility, vector, flux):
    flux[0:SUBS, :] = jnp.zeros((SUBS, LANES), F32)
    flux[geo.base(geo.faces) :, :] = jnp.zeros((SUBS, LANES), F32)
    for z in range(geo.layers):
        v = [vector[z, b] for b in range(3)]
        for a in range(3):
            block = mobility[z, a, 0].astype(F32) * v[0]
            block += mobility[z, a, 1].astype(F32) * v[1]
            block += mobility[z, a, 2].astype(F32) * v[2]
            base = geo.base(3 * z + a)
            flux[base : base + geo.rows, :] = block


def gather_cells(geo, vector, rowp, lanep, finish):
    shape = (SUBS, LANES)
    for g in range(geo.groups):
        lane = spread(lanep[g : g + 1, :], shape)
        row = spread(rowp[g : g + 1, :], shape) - iota(shape, 0)
        kept = [jnp.zeros(shape, F32) for _ in range(3)]
        for z in range(geo.layers):
            for h in range(geo.rows // SUBS):
                mine = row == z * geo.rows + h * SUBS
                for c in range(3):
                    found = take_lanes(vector[z, c, h * SUBS : (h + 1) * SUBS, :], lane)
                    kept[c] = jnp.where(mine, found, kept[c])
        finish(g, kept)


def precondition(geo, inverse, source, target):
    for h in range(geo.layers // 2):
        v = [source(2 * h + f // 3, f % 3) for f in range(6)]
        for e in range(6):
            block = inverse[h, e, 0].astype(F32) * v[0]
            for f in range(1, 6):
                block += inverse[h, e, f].astype(F32) * v[f]
            target(2 * h + e // 3, e % 3, block)


def first_body(geo, *refs):
    far, refs = refs[:7], refs[7:]
    (flux, send, rowp, lanep, spot_hot, hi, lo, inv_dev, inv_pos, turned, guess, mobility, well_in, well_out), refs = refs[:14], refs[14:]
    cells, slots, inverse, wide, ints, packed, sems = refs
    targets = (cells, slots, guess, mobility, inverse, well_in, well_out)
    copies = [pltpu.make_async_copy(source, target, sems.at[i]) for i, (source, target) in enumerate(zip(far, targets))]
    for copy in copies:
        copy.start()
    wide[...] = jnp.zeros_like(wide)
    copies[0].wait()
    wide[:, 0 : geo.cap] = cells[...] + 1
    pack_slots(geo, wide, 0, ints)
    index = ints[...] - 1
    rowp[...] = index >> 7
    lanep[...] = index & (LANES - 1)
    copies[1].wait()
    slot_tables(geo, slots, hi, lo, inv_dev, inv_pos, wide, ints)
    copies[2].wait()
    copies[3].wait()
    write_flux(geo, mobility, guess, flux)
    write_faces(geo, flux, send)
    send[:, 0:LANES] = jnp.zeros((geo.devices, LANES), F32)
    packed[...] = jnp.zeros_like(packed)

    def finish(g, kept):
        for c in range(3):
            packed[c, g : g + 1, :] = jnp.sum(kept[c], axis=0, keepdims=True)

    gather_cells(geo, guess, rowp, lanep, finish)
    for c in range(3):
        unpack_slots(geo, packed[c], c * geo.cap, send)
    for g in range(geo.groups):
        row, lane = rowp[g : g + 1, :], lanep[g : g + 1, :]
        upper = jnp.where(row >= geo.half_rows, LANES, 0)
        spot_hot[:, g * LANES : (g + 1) * LANES] = one_hot(upper + lane, 2 * LANES)
    copies[4].wait()
    for w in range(geo.wells):
        turned[w] = inverse[w].T
    copies[5].wait()
    copies[6].wait()


def slot_tables(geo, slot_ref, hi, lo, inv_dev, inv_pos, wide, packed):
    wide[:, 0 : geo.cap] = slot_ref[...] + 1
    slots = wide[...] - 1
    hi[...] = slots >> 7
    lo[...] = slots & (LANES - 1)
    pack_slots(geo, wide, 0, packed)
    slots = packed[...] - 1
    slot_hi = slots >> 7
    slot_lo = slots & (LANES - 1)
    at = iota((geo.wells, LANES), 1)
    piece = lax.div(at, geo.cap)
    position = (lax.rem(at, geo.cap) + 1).astype(F32)
    found = jnp.zeros((2 * geo.wells, LANES), F32)
    for g in range(geo.groups):
        well = spread(slot_hi[g : g + 1], (geo.wells, LANES)) == iota((geo.wells, LANES), 0)
        device = (piece * geo.groups + (g + 1)).astype(F32)
        marks = jnp.concatenate([jnp.where(well, device, 0.0), jnp.where(well, position, 0.0)], axis=0)
        hot = one_hot(slot_lo[g : g + 1], LANES)
        found += lax.dot_general(marks.astype(BF16), hot, (((1,), (1,)), ((), ())), preferred_element_type=F32)
    inv_dev[...] = found[: geo.wells].astype(jnp.int32) - 1
    inv_pos[...] = jnp.maximum(found[geo.wells :].astype(jnp.int32) - 1, 0)


def relay(geo, came, back):
    shape = (geo.devices, LANES)
    at = iota(shape, 0)
    even = (iota(shape, 1) & 1) == 0
    within = lax.rem(at, geo.n_gy)
    faces = jnp.full(shape, lax.axis_index(AXES), jnp.int32) < geo.faces
    up, down, count = geo.n_gy, geo.devices - geo.n_gy, geo.devices
    one = came[:, LANES : 2 * LANES]
    two = came[:, 2 * LANES : 3 * LANES]
    after = jnp.where(at < down, pltpu.roll(one, down, 0), 0.0)
    before = jnp.where(at >= up, pltpu.roll(two, up, 0), 0.0)

    def beside(block):
        low = jnp.where(within > 0, pltpu.roll(pltpu.roll(block, 1, 1), 1, 0), 0.0)
        high = jnp.where(within < geo.n_gy - 1, pltpu.roll(pltpu.roll(block, LANES - 1, 1), count - 1, 0), 0.0)
        return jnp.where(even, high, low)

    back[:, LANES : 2 * LANES] = jnp.where(faces, after, beside(one))
    back[:, 2 * LANES : 3 * LANES] = jnp.where(faces, before, beside(two))


def at_segments(geo, came, inv_dev, inv_pos, offset):
    shape = (geo.wells, LANES)
    device = inv_dev[...]
    position = inv_pos[...] + offset
    kept = jnp.zeros(shape, F32)
    for s in range(geo.devices):
        found = take_lanes(spread(came[s : s + 1, 0:LANES], shape), position)
        kept = jnp.where(device == s, found, kept)
    return kept


def at_slots(geo, rows, hi, lo):
    shape = (geo.devices, LANES)
    kept = jnp.zeros(shape, F32)
    for w in range(geo.wells):
        found = take_lanes(spread(rows[w], shape), lo)
        kept = jnp.where(hi == w, found, kept)
    return kept


def solve_segments(geo, rate, turned):
    rate_t = rate.T
    rows = []
    for w in range(geo.wells):
        rows.append(jnp.sum(turned[w] * rate_t[:, w : w + 1], axis=0, keepdims=True))
    return rows


def owner_first_body(geo, came, inv_dev, inv_pos, hi_ref, lo_ref, turned, well_in, well_out, back):
    hi, lo = hi_ref[...], lo_ref[...]
    rows_in = [[well_in[c : c + 1, w * LANES : (w + 1) * LANES] for w in range(geo.wells)] for c in range(3)]
    rows_out = [[well_out[c : c + 1, w * LANES : (w + 1) * LANES] for w in range(geo.wells)] for c in range(3)]
    rate = jnp.zeros((geo.wells, LANES), F32)
    for c in range(3):
        rate += jnp.concatenate(rows_in[c], axis=0) * at_segments(geo, came, inv_dev, inv_pos, c * geo.cap)
    back[:, 0:LANES] = at_slots(geo, solve_segments(geo, rate, turned), hi, lo)
    relay(geo, came, back)
    for place, rows in ((3, rows_in), (4, rows_out)):
        block = jnp.zeros((geo.devices, LANES), F32)
        for c in range(3):
            part = at_slots(geo, rows[c], hi, lo)
            block += pltpu.roll(part, c * geo.cap, 1) if c else part
        back[:, place * LANES : (place + 1) * LANES] = block


def owner_body(geo, came, inv_dev, inv_pos, hi_ref, lo_ref, turned, back, sums):
    rate = at_segments(geo, came, inv_dev, inv_pos, 0)
    back[:, 0:LANES] = at_slots(geo, solve_segments(geo, rate, turned), hi_ref[...], lo_ref[...])
    relay(geo, came, back)
    sums[...] = spread(jnp.sum(came[:, 0:LANES], axis=0, keepdims=True), sums.shape)


def scatter_terms(geo, came, coeff_out, rowp, spot_hot, packed, left, spots):
    pack_slots(geo, came, 0, packed)
    rate = packed[...]
    parts = []
    for c in range(3):
        value = coeff_out[c] * rate
        high = value.astype(BF16)
        parts += [high, (value - high.astype(F32)).astype(BF16)]
    n = geo.half_rows
    row = rowp[...]
    row = jnp.where(row >= n, row - n, row)
    for g in range(geo.groups):
        hot = one_hot(row[g : g + 1], n)
        for i, part in enumerate(parts):
            left[i * n : (i + 1) * n, g * LANES : (g + 1) * LANES] = hot * spread(part[g : g + 1], hot.shape)
    result = lax.dot_general(left[...], spot_hot[...], (((1,), (1,)), ((), ())), preferred_element_type=F32)
    for c in range(3):
        i = 2 * c * n
        summed = result[i : i + n] + result[i + n : i + 2 * n]
        for h in range(2):
            low = c * geo.tile_rows + h * n
            spots[low : low + n, :] = summed[:, h * LANES : (h + 1) * LANES]


def apply_operator(geo, came, vector, flux, diag, face, spots, store):
    at_row, at_lane = iota((SUBS, LANES), 0), iota(geo.tile, 1)
    one, two, three = LANES, 2 * LANES, 3 * LANES
    last = geo.faces + SUBS
    edges = jnp.concatenate([came[geo.faces : last, one:two], came[geo.faces : last, two:three]], axis=0)
    for z in range(geo.layers):
        f = [face[n, z].astype(F32) for n in range(6)]
        v = [vector[z, b] for b in range(3)]
        for a in range(3):
            j = 3 * z + a
            base = geo.base(j)
            block = flux[base : base + geo.rows, :]
            first = jnp.where(at_row == 0, spread(came[j : j + 1, two:three], at_row.shape), flux[base - 1 : base - 1 + SUBS, :])
            under = jnp.concatenate([first, flux[base - 1 + SUBS : base - 1 + geo.rows, :]], axis=0)
            final = jnp.where(at_row == SUBS - 1, spread(came[j : j + 1, one:two], at_row.shape), flux[base + 1 + SUBS : base + 1 + geo.rows, :])
            over = jnp.concatenate([flux[base + 1 : base + 1 + SUBS, :], final], axis=0)
            ends = pltpu.roll(edges, LANES - 1 - 2 * j, 1)
            left = jnp.where(at_lane == 0, ends, pltpu.roll(block, 1, 1))
            right = jnp.where(at_lane == LANES - 1, ends, pltpu.roll(block, LANES - 1, 1))
            beside = f[0] * under + f[1] * over + f[2] * left + f[3] * right
            if z > 0:
                beside += f[4] * flux[base - 3 * geo.rows : base - 2 * geo.rows, :]
            if z + 1 < geo.layers:
                beside += f[5] * flux[base + 3 * geo.rows : base + 4 * geo.rows, :]
            own = diag[z, a, 0].astype(F32) * v[0]
            own += diag[z, a, 1].astype(F32) * v[1]
            own += diag[z, a, 2].astype(F32) * v[2]
            low = a * geo.tile_rows + z * geo.rows
            store(z, a, own - beside - spots[low : low + geo.rows, :])


def send_next(geo, source, inverse, mobility, rowp, lanep, coeff_in, dots, ahead, flux, send, packed):
    def put(z, c, block):
        ahead[z, c] = block

    precondition(geo, inverse, lambda z, c: source[z, c], put)
    write_flux(geo, mobility, ahead, flux)
    write_faces(geo, flux, send)
    at = iota((1, LANES), 1)
    row = jnp.zeros((1, LANES), F32)
    for n, dot in enumerate(dots):
        row = jnp.where(at == geo.cap + n, spread(total(dot), (1, LANES)), row)
    send[:, 0:LANES] = spread(row, (geo.devices, LANES))
    packed[...] = jnp.zeros_like(packed)

    def finish(g, kept):
        rate = kept[0] * spread(coeff_in[0, g : g + 1, :], kept[0].shape)
        rate += kept[1] * spread(coeff_in[1, g : g + 1, :], kept[0].shape)
        rate += kept[2] * spread(coeff_in[2, g : g + 1, :], kept[0].shape)
        packed[g : g + 1, :] = jnp.sum(rate, axis=0, keepdims=True)

    gather_cells(geo, ahead, rowp, lanep, finish)
    unpack_slots(geo, packed[...], 0, send)


def stage_body(geo, rule, n_in, n_out, goes_on, *refs):
    refs = list(refs)

    def take(n):
        got, refs[:n] = refs[:n], []
        return got

    came, vector, flux_in, rowp, lanep, spot_hot = take(6)
    inputs = take(n_in)
    diag, face, *hats = take(4 if goes_on else 2)
    outputs = take(n_out)
    following = take(3) if goes_on else take(1)
    packed, left, spots = take(3)
    coeff_in, coeff_out, store, source, dots = rule(came, packed, inputs, outputs)
    scatter_terms(geo, came, coeff_out, rowp, spot_hot, packed, left, spots)
    apply_operator(geo, came, vector, flux_in, diag, face, spots, store)
    if goes_on:
        ahead, flux, send = following
        send_next(geo, source, *hats, rowp, lanep, coeff_in, dots, ahead, flux, send, packed)
    else:
        at = iota((1, LANES), 1)
        row = jnp.where(at == 0, spread(total(dots[0]), (1, LANES)), spread(total(dots[1]), (1, LANES)))
        following[0][...] = spread(row, following[0].shape)


def zeros(geo, count):
    return [jnp.zeros(geo.tile, F32) for _ in range(count)]


def pick(sums, geo, n):
    return sums[0:1, geo.cap + n : geo.cap + n + 1]


def keep(ref, value):
    ref[...] = spread(value, ref.shape)


def residual_rule(geo, came, packed, inputs, outputs):
    (right_side,) = inputs
    shadow, coeff_in, coeff_out = outputs
    for c in range(3):
        pack_slots(geo, came, 3 * LANES + c * geo.cap, packed)
        coeff_in[c] = packed[...]
        pack_slots(geo, came, 4 * LANES + c * geo.cap, packed)
        coeff_out[c] = packed[...]
    dots = zeros(geo, 1)

    def store(z, c, image):
        value = right_side[z, c] - image
        shadow[z, c] = value
        dots[0] += value * value

    return coeff_in, coeff_out, store, shadow, dots


def image_rule(geo, came, packed, inputs, outputs):
    coeff_in, coeff_out, shadow = inputs
    (applied,) = outputs
    dots = zeros(geo, 1)

    def store(z, c, image):
        applied[z, c] = image
        dots[0] += shadow[z, c] * image

    return coeff_in, coeff_out, store, applied, dots


def half_rule(geo, came, packed, inputs, outputs):
    coeff_in, coeff_out, shadow, rho_sums, rho_at, sums, residual, applied, behind = inputs
    step_out, deeper, half, response = outputs
    step = rho_sums[0:1, rho_at : rho_at + 1] / pick(sums, geo, 0)
    keep(step_out, step)
    step = spread(step, geo.tile)
    dots = zeros(geo, 4)

    def store(z, c, image):
        deeper[z, c] = image
        s = residual[z, c] - step * applied[z, c]
        t = behind[z, c] - step * image
        half[z, c] = s
        response[z, c] = t
        dots[0] += t * s
        dots[1] += t * t
        dots[2] += shadow[z, c] * t
        dots[3] += shadow[z, c] * s

    return coeff_in, coeff_out, store, response, dots


def next_rule(geo, came, packed, inputs, outputs):
    coeff_in, coeff_out, shadow, rho_sums, rho_at, step_in, sums, half, response, applied, deeper, search, moved = inputs
    rho_out, residual_next, behind_next, applied_next, search_next, moved_next = outputs
    smoothing = pick(sums, geo, 0) / pick(sums, geo, 1)
    rho_next = pick(sums, geo, 3) - smoothing * pick(sums, geo, 2)
    step = step_in[0:1, 0:1]
    momentum = (rho_next / rho_sums[0:1, rho_at : rho_at + 1]) * (step / smoothing)
    keep(rho_out, rho_next)
    smoothing, momentum, step = (spread(x, geo.tile) for x in (smoothing, momentum, step))
    dots = zeros(geo, 1)

    def store(z, c, image):
        t = response[z, c]
        s = half[z, c]
        p = search[z, c]
        v = applied[z, c]
        r = s - smoothing * t
        w = t - smoothing * image
        v_next = w + momentum * (v - smoothing * deeper[z, c])
        residual_next[z, c] = r
        behind_next[z, c] = w
        applied_next[z, c] = v_next
        search_next[z, c] = r + momentum * (p - smoothing * v)
        by = step * p + smoothing * s
        moved_next[z, c] = by if moved is None else moved[z, c] + by
        dots[0] += shadow[z, c] * v_next

    return coeff_in, coeff_out, store, applied_next, dots


def last_rule(geo, came, packed, inputs, outputs):
    coeff_out, rho_sums, rho_at, sums, residual, applied, behind, search, moved = inputs
    half, response, moved_next = outputs
    step = spread(rho_sums[0:1, rho_at : rho_at + 1] / pick(sums, geo, 0), geo.tile)
    dots = zeros(geo, 2)

    def store(z, c, image):
        s = residual[z, c] - step * applied[z, c]
        t = behind[z, c] - step * image
        half[z, c] = s
        response[z, c] = t
        by = step * search[z, c]
        moved_next[z, c] = by if moved is None else moved[z, c] + by
        dots[0] += t * s
        dots[1] += t * t

    return None, coeff_out, store, None, dots


def finish_body(geo, came, moved, half, response, guess, inverse, solution_out, residual_out, solution, residual, sems):
    sums = jnp.sum(came[...], axis=0, keepdims=True)
    smoothing = spread(sums[:, 0:1] / sums[:, 1:2], geo.tile)
    copies = []

    def leave(source, target, layer, sem):
        copies.append(pltpu.make_async_copy(source.at[layer], target.at[layer], sem))
        copies[-1].start()

    for z, c in geo.tiles():
        residual[z, c] = half[z, c] - smoothing * response[z, c]
        if c + 1 == geo.comps:
            leave(residual, residual_out, z, sems.at[0, z])

    def put(z, c, block):
        solution[z, c] = guess[z, c] + block
        if z % 2 and c + 1 == geo.comps:
            leave(solution, solution_out, z - 1, sems.at[1, z - 1])
            leave(solution, solution_out, z, sems.at[1, z])

    precondition(geo, inverse, lambda z, c: moved[z, c] + smoothing * half[z, c], put)
    for copy in copies:
        copy.wait()


def exchange(rows):
    return lax.all_to_all(rows, AXES, split_axis=0, concat_axis=0, tiled=True)


def per_device(right_side, guess, diag, mobility, face, inverse, perf_cell, perf_slot, well_in, well_out, well_inverse):
    geo = Geometry(right_side.shape, perf_cell.shape[1:], well_inverse.shape, lax.axis_size("gy"))
    ints = jnp.int32
    block = (geo.devices, LANES)
    packed = (geo.groups_pad, LANES)
    seg = (geo.wells, LANES)
    wide = ((geo.devices, 3 * LANES), F32)
    small = ((SUBS, LANES), F32)
    vec = (geo.vector, F32)
    coeffs = ((3,) + packed, F32)
    sent = [vec, (geo.flux, F32), wide]

    table = (perf_cell.shape[1:], ints)
    flux, send, rowp, lanep, spot_hot, hi, lo, inv_dev, inv_pos, turned, guess_held, mobility, well_in, well_out = call(
        functools.partial(first_body, geo),
        [(geo.flux, F32), wide, (packed, ints), (packed, ints), ((2 * LANES, geo.slots), BF16), (block, ints), (block, ints),
         (seg, ints), (seg, ints), (well_inverse.shape, F32), vec, (mobility.shape, BF16), (well_in.shape, F32), (well_out.shape, F32)],
        [], far=[perf_cell[0], perf_slot[0], guess, mobility, well_inverse, well_in, well_out],
        scratch=[pltpu.VMEM(*table), pltpu.VMEM(*table), pltpu.VMEM(well_inverse.shape, F32), pltpu.VMEM(block, ints),
                 pltpu.VMEM(packed, ints), pltpu.VMEM((3,) + packed, F32), pltpu.SemaphoreType.DMA((7,))],
    )
    owner_tables = [inv_dev, inv_pos, hi, lo, turned]
    scratch = [pltpu.VMEM(packed, F32), pltpu.VMEM((6 * geo.half_rows, geo.slots), BF16), pltpu.VMEM((3 * geo.tile_rows, LANES), F32)]

    def stage(rule, outs, came, vector, flux, inputs, goes_on=True):
        arrays = [i for i in inputs if i is not None and not isinstance(i, int)]

        def placed(came, packed, refs, out_refs):
            rest = list(refs)
            return rule(geo, came, packed, [i if i is None or isinstance(i, int) else rest.pop(0) for i in inputs], out_refs)

        return call(
            functools.partial(stage_body, geo, placed, len(arrays), len(outs), goes_on),
            outs + (sent if goes_on else [(block, F32)]),
            [came, vector, flux, rowp, lanep, spot_hot] + arrays + [diag, face] + ([inverse, mobility] if goes_on else []), scratch=scratch,
        )

    def owner(send):
        back, sums = call(functools.partial(owner_body, geo), [wide, small], [exchange(send)] + owner_tables)
        return exchange(back), sums

    (back,) = call(
        functools.partial(owner_first_body, geo), [((geo.devices, 5 * LANES), F32)], [exchange(send)] + owner_tables + [well_in, well_out]
    )
    shadow, coeff_in, coeff_out, ahead, flux, send = stage(residual_rule, [vec, coeffs, coeffs], exchange(back), guess_held, flux, [right_side])
    always = [coeff_in, coeff_out, shadow]
    came, sums = owner(send)
    rho, rho_at = sums, geo.cap
    applied, ahead, flux, send = stage(image_rule, [vec], came, ahead, flux, always)
    residual, search, behind, moved = shadow, shadow, applied, None
    for iteration in range(ITERS):
        came, sums = owner(send)
        if iteration + 1 == ITERS:
            half, response, moved, send = stage(
                last_rule, [vec] * 3, came, ahead, flux,
                [coeff_out, rho, rho_at, sums, residual, applied, behind, search, moved], goes_on=False,
            )
            break
        step, deeper, half, response, ahead, flux, send = stage(
            half_rule, [small] + [vec] * 3, came, ahead, flux, always + [rho, rho_at, sums, residual, applied, behind]
        )
        came, sums = owner(send)
        rho, residual, behind, applied, search, moved, ahead, flux, send = stage(
            next_rule, [small] + [vec] * 5, came, ahead, flux,
            always + [rho, rho_at, step, sums, half, response, applied, deeper, search, moved],
        )
        rho_at = 0
    return call(
        functools.partial(finish_body, geo), [vec] * 2, [exchange(send), moved, half, response, guess, inverse],
        scratch=[pltpu.VMEM(*vec), pltpu.VMEM(*vec), pltpu.SemaphoreType.DMA((2, geo.layers))], out_far=True,
    )


def solution(mesh):
    in_specs = (
        P(None, None, "gx", "gy"),
        P(None, None, "gx", "gy"),
        P(None, None, None, "gx", "gy"),
        P(None, None, None, "gx", "gy"),
        P(None, None, "gx", "gy"),
        P(None, None, None, "gx", "gy"),
        P(AXES, None, None),
        P(AXES, None, None),
        P(None, AXES),
        P(None, AXES),
        P(AXES, None, None),
    )
    out_specs = (P(None, None, "gx", "gy"), P(None, None, "gx", "gy"))
    return jax.shard_map(per_device, mesh=mesh, in_specs=in_specs, out_specs=out_specs, check_vma=False)
```

```python
import functools

import jax
import jax.numpy as jnp
from jax import lax
from jax.experimental import pallas as pl
from jax.experimental.pallas import tpu as pltpu
from jax.sharding import PartitionSpec as P

ITERS = 2
AXES = ("gx", "gy")
LANES = 128
SUBS = 8
F32 = jnp.float32
BF16 = jnp.bfloat16
SCOPED = 16 * 1024 * 1024


class Geometry:
    def __init__(self, vector_shape, table_shape, inverse_shape, n_gy):
        self.layers, self.comps, self.rows, self.cols = vector_shape
        self.devices, self.cap = table_shape
        self.wells, self.segs = inverse_shape[:2]
        self.n_gy = n_gy
        self.tile_rows = self.layers * self.rows
        self.half_rows = self.tile_rows // 2
        self.faces = self.layers * self.comps
        self.per = LANES // self.cap
        self.groups = -(-self.devices // self.per)
        self.groups_pad = -(-self.groups // SUBS) * SUBS
        self.slots = self.groups * LANES
        self.vector = (self.layers, self.comps, self.rows, self.cols)
        self.flux = (self.faces * self.rows + 2 * SUBS, self.cols)
        self.tile = (self.rows, LANES)
        assert self.cols == LANES and self.segs == LANES and self.rows == 2 * SUBS
        assert self.faces + SUBS <= self.devices and 2 * self.faces <= LANES
        assert 3 * self.cap <= LANES

    def pieces(self):
        for k in range(self.per):
            low = k * self.groups
            count = min(self.groups, self.devices - low)
            if count > 0:
                yield k, low, count

    def tiles(self):
        for z in range(self.layers):
            for c in range(self.comps):
                yield z, c

    def base(self, j):
        return SUBS + j * self.rows


HELD = pl.BlockSpec(memory_space=pltpu.VMEM)
FAR = pl.BlockSpec(memory_space=pltpu.HBM)


def call(body, outs, args, far=(), scratch=(), out_far=False):
    held = [pltpu.with_memory_space_constraint(a, pltpu.VMEM) for a in args]
    far = [pltpu.with_memory_space_constraint(a, pltpu.HBM) for a in far]
    shapes = [jax.ShapeDtypeStruct(*o) if out_far else pltpu.VMEM(*o) for o in outs]
    return pl.pallas_call(
        body,
        out_shape=tuple(shapes),
        in_specs=[HELD] * len(held) + [FAR] * len(far),
        out_specs=(FAR if out_far else HELD,) * len(outs),
        scratch_shapes=list(scratch),
        compiler_params=pltpu.CompilerParams(vmem_limit_bytes=SCOPED),
    )(*held, *far)


class Rows:
    def __init__(self, ref, width):
        self.ref, self.width = ref, width
        self.devices = ref.shape[0] // width

    def at(self, k, low=0, count=None):
        count = self.devices - low if count is None else count
        start = low * self.width + k
        if self.width == 1 or count == 1:
            return (slice(start, start + count), slice(None))
        return (pl.ds(start, count, stride=self.width), slice(None))

    def get(self, k, low=0, count=None):
        return self.ref[self.at(k, low, count)]

    def put(self, k, value, low=0):
        self.ref[self.at(k, low, value.shape[0])] = value


def iota(shape, dim):
    return lax.broadcasted_iota(jnp.int32, shape, dim)


def take_lanes(table, index):
    return jnp.take_along_axis(table, index, axis=1, mode="promise_in_bounds")


def spread(row, shape):
    return jnp.broadcast_to(row, shape)


def total(block):
    return jnp.sum(jnp.sum(block, axis=0, keepdims=True), axis=1, keepdims=True)


def one_hot(index, size):
    rows = spread(index, (size, LANES))
    return jnp.where(rows == iota(rows.shape, 0), 1.0, 0.0).astype(BF16)


def pack_slots(geo, rows, at_row, lane, packed_ref):
    packed_ref[...] = jnp.zeros_like(packed_ref)
    for k, low, count in geo.pieces():
        part = rows.get(at_row, low, count)
        shift = (k * geo.cap - lane) % LANES
        part = pltpu.roll(part, shift, 1) if shift else part
        at = iota(part.shape, 1)
        mine = (at >= k * geo.cap) & (at < (k + 1) * geo.cap)
        packed_ref[0:count, :] = jnp.where(mine, part, packed_ref[0:count, :])


def unpack_slots(geo, packed, lane, rows):
    for k, low, count in geo.pieces():
        shift = (lane - k * geo.cap) % LANES
        part = pltpu.roll(packed, shift, 1) if shift else packed
        part = part[0:count]
        at = iota(part.shape, 1)
        mine = (at >= lane) & (at < lane + geo.cap)
        rows.put(0, jnp.where(mine, part, rows.get(0, low, count)), low)


def write_faces(geo, flux, send):
    if geo.devices > geo.faces + SUBS:
        nothing = jnp.zeros((geo.devices - geo.faces - SUBS, LANES), F32)
        send.put(1, nothing, geo.faces + SUBS)
        send.put(2, nothing, geo.faces + SUBS)
    send.put(1, flux[pl.ds(geo.base(0), geo.faces, stride=geo.rows), :])
    send.put(2, flux[pl.ds(geo.base(0) + geo.rows - 1, geo.faces, stride=geo.rows), :])
    at = iota(geo.tile, 1) >> 1
    edges = jnp.zeros(geo.tile, F32)
    for j in range(geo.faces):
        turned = pltpu.roll(flux[geo.base(j) : geo.base(j) + geo.rows, :], 2 * j + 1, 1)
        edges = jnp.where(at == j, turned, edges)
    send.put(1, edges[:SUBS], geo.faces)
    send.put(2, edges[SUBS:], geo.faces)


def write_flux(geo, mobility, vector, flux):
    flux[0:SUBS, :] = jnp.zeros((SUBS, LANES), F32)
    flux[geo.base(geo.faces) :, :] = jnp.zeros((SUBS, LANES), F32)
    for z in range(geo.layers):
        v = [vector[z, b] for b in range(3)]
        for a in range(3):
            block = mobility[z, a, 0].astype(F32) * v[0]
            block += mobility[z, a, 1].astype(F32) * v[1]
            block += mobility[z, a, 2].astype(F32) * v[2]
            base = geo.base(3 * z + a)
            flux[base : base + geo.rows, :] = block


def gather_cells(geo, vector, rowp, lanep, finish):
    shape = (SUBS, LANES)
    for g in range(geo.groups):
        lane = spread(lanep[g : g + 1, :], shape)
        row = spread(rowp[g : g + 1, :], shape) - iota(shape, 0)
        kept = [jnp.zeros(shape, F32) for _ in range(3)]
        for z in range(geo.layers):
            for h in range(geo.rows // SUBS):
                mine = row == z * geo.rows + h * SUBS
                for c in range(3):
                    found = take_lanes(vector[z, c, h * SUBS : (h + 1) * SUBS, :], lane)
                    kept[c] = jnp.where(mine, found, kept[c])
        finish(g, kept)


def precondition(geo, inverse, source, target):
    for h in range(geo.layers // 2):
        v = [source(2 * h + f // 3, f % 3) for f in range(6)]
        for e in range(6):
            block = inverse[h, e, 0].astype(F32) * v[0]
            for f in range(1, 6):
                block += inverse[h, e, f].astype(F32) * v[f]
            target(2 * h + e // 3, e % 3, block)


def first_body(geo, *refs):
    far, refs = refs[:7], refs[7:]
    (flux, send, rowp, lanep, spot_hot, hi, lo, inv_dev, inv_pos, inverse_held, guess, mobility, well_in, well_out), refs = refs[:14], refs[14:]
    cells, slots, wide, ints, packed, sems = refs
    send = Rows(send, 3)
    targets = (cells, slots, guess, mobility, inverse_held, well_in, well_out)
    copies = [pltpu.make_async_copy(source, target, sems.at[i]) for i, (source, target) in enumerate(zip(far, targets))]
    for copy in copies:
        copy.start()
    wide[...] = jnp.zeros_like(wide)
    copies[0].wait()
    wide[:, 0 : geo.cap] = cells[...] + 1
    pack_slots(geo, Rows(wide, 1), 0, 0, ints)
    index = ints[...] - 1
    rowp[...] = index >> 7
    lanep[...] = index & (LANES - 1)
    copies[1].wait()
    slot_tables(geo, slots, hi, lo, inv_dev, inv_pos, wide, ints)
    copies[2].wait()
    copies[3].wait()
    write_flux(geo, mobility, guess, flux)
    write_faces(geo, flux, send)
    send.put(0, jnp.zeros((geo.devices, LANES), F32))
    packed[...] = jnp.zeros_like(packed)

    def finish(g, kept):
        for c in range(3):
            packed[c, g : g + 1, :] = jnp.sum(kept[c], axis=0, keepdims=True)

    gather_cells(geo, guess, rowp, lanep, finish)
    for c in range(3):
        unpack_slots(geo, packed[c], c * geo.cap, send)
    for g in range(geo.groups):
        row, lane = rowp[g : g + 1, :], lanep[g : g + 1, :]
        upper = jnp.where(row >= geo.half_rows, LANES, 0)
        spot_hot[:, g * LANES : (g + 1) * LANES] = one_hot(upper + lane, 2 * LANES)
    for copy in copies[4:]:
        copy.wait()


def slot_tables(geo, slot_ref, hi, lo, inv_dev, inv_pos, wide, packed):
    wide[:, 0 : geo.cap] = slot_ref[...] + 1
    slots = wide[...] - 1
    hi[...] = slots >> 7
    lo[...] = slots & (LANES - 1)
    pack_slots(geo, Rows(wide, 1), 0, 0, packed)
    slots = packed[...] - 1
    slot_hi = slots >> 7
    slot_lo = slots & (LANES - 1)
    at = iota((geo.wells, LANES), 1)
    piece = lax.div(at, geo.cap)
    position = (lax.rem(at, geo.cap) + 1).astype(F32)
    found = jnp.zeros((2 * geo.wells, LANES), F32)
    for g in range(geo.groups):
        well = spread(slot_hi[g : g + 1], (geo.wells, LANES)) == iota((geo.wells, LANES), 0)
        device = (piece * geo.groups + (g + 1)).astype(F32)
        marks = jnp.concatenate([jnp.where(well, device, 0.0), jnp.where(well, position, 0.0)], axis=0)
        hot = one_hot(slot_lo[g : g + 1], LANES)
        found += lax.dot_general(marks.astype(BF16), hot, (((1,), (1,)), ((), ())), preferred_element_type=F32)
    inv_dev[...] = found[: geo.wells].astype(jnp.int32) - 1
    inv_pos[...] = jnp.maximum(found[geo.wells :].astype(jnp.int32) - 1, 0)


def relay(geo, came, back):
    shape = (geo.devices, LANES)
    at = iota(shape, 0)
    even = (iota(shape, 1) & 1) == 0
    within = lax.rem(at, geo.n_gy)
    faces = jnp.full(shape, lax.axis_index(AXES), jnp.int32) < geo.faces
    up, down, count = geo.n_gy, geo.devices - geo.n_gy, geo.devices
    one, two = came.get(1), came.get(2)
    after = jnp.where(at < down, pltpu.roll(one, down, 0), 0.0)
    before = jnp.where(at >= up, pltpu.roll(two, up, 0), 0.0)

    def beside(block):
        low = jnp.where(within > 0, pltpu.roll(pltpu.roll(block, 1, 1), 1, 0), 0.0)
        high = jnp.where(within < geo.n_gy - 1, pltpu.roll(pltpu.roll(block, LANES - 1, 1), count - 1, 0), 0.0)
        return jnp.where(even, high, low)

    back.put(1, jnp.where(faces, after, beside(one)))
    back.put(2, jnp.where(faces, before, beside(two)))


def at_segments(geo, came, inv_dev, inv_pos, offset):
    shape = (geo.wells, LANES)
    device = inv_dev[...]
    position = inv_pos[...] + offset
    kept = jnp.zeros(shape, F32)
    for s in range(geo.devices):
        found = take_lanes(spread(came.get(0, s, 1), shape), position)
        kept = jnp.where(device == s, found, kept)
    return kept


def at_slots(geo, rows, hi, lo):
    shape = (geo.devices, LANES)
    kept = jnp.zeros(shape, F32)
    for w in range(geo.wells):
        found = take_lanes(spread(rows[w], shape), lo)
        kept = jnp.where(hi == w, found, kept)
    return kept


def solve_segments(geo, rate, inverse):
    shape = (geo.segs, LANES)
    own = iota(shape, 0) == iota(shape, 1)
    rows = []
    for w in range(geo.wells):
        sums = jnp.sum(inverse[w] * rate[w : w + 1, :], axis=1, keepdims=True)
        rows.append(jnp.sum(jnp.where(own, spread(sums, shape), 0.0), axis=0, keepdims=True))
    return rows


def owner_first_body(geo, came, inv_dev, inv_pos, hi_ref, lo_ref, inverse_held, well_in, well_out, back):
    came, back = Rows(came, 3), Rows(back, 5)
    hi, lo = hi_ref[...], lo_ref[...]
    rows_in = [[well_in[c : c + 1, w * LANES : (w + 1) * LANES] for w in range(geo.wells)] for c in range(3)]
    rows_out = [[well_out[c : c + 1, w * LANES : (w + 1) * LANES] for w in range(geo.wells)] for c in range(3)]
    rate = jnp.zeros((geo.wells, LANES), F32)
    for c in range(3):
        rate += jnp.concatenate(rows_in[c], axis=0) * at_segments(geo, came, inv_dev, inv_pos, c * geo.cap)
    back.put(0, at_slots(geo, solve_segments(geo, rate, inverse_held), hi, lo))
    relay(geo, came, back)
    for place, rows in ((3, rows_in), (4, rows_out)):
        block = jnp.zeros((geo.devices, LANES), F32)
        for c in range(3):
            part = at_slots(geo, rows[c], hi, lo)
            block += pltpu.roll(part, c * geo.cap, 1) if c else part
        back.put(place, block)


def owner_body(geo, came, inv_dev, inv_pos, hi_ref, lo_ref, inverse_held, back, sums):
    came, back = Rows(came, 3), Rows(back, 3)
    rate = at_segments(geo, came, inv_dev, inv_pos, 0)
    back.put(0, at_slots(geo, solve_segments(geo, rate, inverse_held), hi_ref[...], lo_ref[...]))
    relay(geo, came, back)
    sums[...] = spread(jnp.sum(came.get(0), axis=0, keepdims=True), sums.shape)


def scatter_terms(geo, came, coeff_out, rowp, spot_hot, packed, left, spots):
    pack_slots(geo, came, 0, 0, packed)
    rate = packed[...]
    parts = []
    for c in range(3):
        value = coeff_out[c] * rate
        high = value.astype(BF16)
        parts += [high, (value - high.astype(F32)).astype(BF16)]
    n = geo.half_rows
    row = rowp[...]
    row = jnp.where(row >= n, row - n, row)
    for g in range(geo.groups):
        hot = one_hot(row[g : g + 1], n)
        for i, part in enumerate(parts):
            left[i * n : (i + 1) * n, g * LANES : (g + 1) * LANES] = hot * spread(part[g : g + 1], hot.shape)
    result = lax.dot_general(left[...], spot_hot[...], (((1,), (1,)), ((), ())), preferred_element_type=F32)
    for c in range(3):
        i = 2 * c * n
        summed = result[i : i + n] + result[i + n : i + 2 * n]
        for h in range(2):
            low = c * geo.tile_rows + h * n
            spots[low : low + n, :] = summed[:, h * LANES : (h + 1) * LANES]


def apply_operator(geo, came, vector, flux, diag, face, spots, store):
    at_row, at_lane = iota((SUBS, LANES), 0), iota(geo.tile, 1)
    edges = jnp.concatenate([came.get(1, geo.faces, SUBS), came.get(2, geo.faces, SUBS)], axis=0)
    for z in range(geo.layers):
        f = [face[n, z].astype(F32) for n in range(6)]
        v = [vector[z, b] for b in range(3)]
        for a in range(3):
            j = 3 * z + a
            base = geo.base(j)
            block = flux[base : base + geo.rows, :]
            first = jnp.where(at_row == 0, spread(came.get(2, j, 1), at_row.shape), flux[base - 1 : base - 1 + SUBS, :])
            under = jnp.concatenate([first, flux[base - 1 + SUBS : base - 1 + geo.rows, :]], axis=0)
            final = jnp.where(at_row == SUBS - 1, spread(came.get(1, j, 1), at_row.shape), flux[base + 1 + SUBS : base + 1 + geo.rows, :])
            over = jnp.concatenate([flux[base + 1 : base + 1 + SUBS, :], final], axis=0)
            ends = pltpu.roll(edges, LANES - 1 - 2 * j, 1)
            left = jnp.where(at_lane == 0, ends, pltpu.roll(block, 1, 1))
            right = jnp.where(at_lane == LANES - 1, ends, pltpu.roll(block, LANES - 1, 1))
            beside = f[0] * under + f[1] * over + f[2] * left + f[3] * right
            if z > 0:
                beside += f[4] * flux[base - 3 * geo.rows : base - 2 * geo.rows, :]
            if z + 1 < geo.layers:
                beside += f[5] * flux[base + 3 * geo.rows : base + 4 * geo.rows, :]
            own = diag[z, a, 0].astype(F32) * v[0]
            own += diag[z, a, 1].astype(F32) * v[1]
            own += diag[z, a, 2].astype(F32) * v[2]
            low = a * geo.tile_rows + z * geo.rows
            store(z, a, own - beside - spots[low : low + geo.rows, :])


def send_next(geo, source, inverse, mobility, rowp, lanep, coeff_in, dots, ahead, flux, send, packed):
    def put(z, c, block):
        ahead[z, c] = block

    precondition(geo, inverse, lambda z, c: source[z, c], put)
    at = iota((1, LANES), 1)
    row = jnp.zeros((1, LANES), F32)
    for n, dot in enumerate(dots):
        row = jnp.where(at == geo.cap + n, spread(total(dot), (1, LANES)), row)
    send.put(0, spread(row, (geo.devices, LANES)))
    packed[...] = jnp.zeros_like(packed)

    def finish(g, kept):
        rate = kept[0] * spread(coeff_in[0, g : g + 1, :], kept[0].shape)
        rate += kept[1] * spread(coeff_in[1, g : g + 1, :], kept[0].shape)
        rate += kept[2] * spread(coeff_in[2, g : g + 1, :], kept[0].shape)
        packed[g : g + 1, :] = jnp.sum(rate, axis=0, keepdims=True)

    gather_cells(geo, ahead, rowp, lanep, finish)
    write_flux(geo, mobility, ahead, flux)
    write_faces(geo, flux, send)
    unpack_slots(geo, packed[...], 0, send)


def stage_body(geo, rule, n_in, n_out, goes_on, *refs):
    refs = list(refs)

    def take(n):
        got, refs[:n] = refs[:n], []
        return got

    came, vector, flux_in, rowp, lanep, spot_hot = take(6)
    inputs = take(n_in)
    diag, face, *hats = take(4 if goes_on else 2)
    outputs = take(n_out)
    following = take(3) if goes_on else take(1)
    packed, left, spots = take(3)
    came = Rows(came, came.shape[0] // geo.devices)
    coeff_in, coeff_out, store, source, dots = rule(came, packed, inputs, outputs)
    scatter_terms(geo, came, coeff_out, rowp, spot_hot, packed, left, spots)
    apply_operator(geo, came, vector, flux_in, diag, face, spots, store)
    if goes_on:
        ahead, flux, send = following
        send = Rows(send, 3)
        send_next(geo, source, *hats, rowp, lanep, coeff_in, dots, ahead, flux, send, packed)
    else:
        at = iota((1, LANES), 1)
        row = jnp.where(at == 0, spread(total(dots[0]), (1, LANES)), spread(total(dots[1]), (1, LANES)))
        following[0][...] = spread(row, following[0].shape)


def zeros(geo, count):
    return [jnp.zeros(geo.tile, F32) for _ in range(count)]


def pick(sums, geo, n):
    return sums[0:1, geo.cap + n : geo.cap + n + 1]


def keep(ref, value):
    ref[...] = spread(value, ref.shape)


def residual_rule(geo, came, packed, inputs, outputs):
    (right_side,) = inputs
    shadow, coeff_in, coeff_out = outputs
    for c in range(3):
        pack_slots(geo, came, 3, c * geo.cap, packed)
        coeff_in[c] = packed[...]
        pack_slots(geo, came, 4, c * geo.cap, packed)
        coeff_out[c] = packed[...]
    dots = zeros(geo, 1)

    def store(z, c, image):
        value = right_side[z, c] - image
        shadow[z, c] = value
        dots[0] += value * value

    return coeff_in, coeff_out, store, shadow, dots


def image_rule(geo, came, packed, inputs, outputs):
    coeff_in, coeff_out, shadow = inputs
    (applied,) = outputs
    dots = zeros(geo, 1)

    def store(z, c, image):
        applied[z, c] = image
        dots[0] += shadow[z, c] * image

    return coeff_in, coeff_out, store, applied, dots


def half_rule(geo, came, packed, inputs, outputs):
    coeff_in, coeff_out, shadow, rho_sums, rho_at, sums, residual, applied, behind = inputs
    step_out, deeper, half, response = outputs
    step = rho_sums[0:1, rho_at : rho_at + 1] / pick(sums, geo, 0)
    keep(step_out, step)
    step = spread(step, geo.tile)
    dots = zeros(geo, 4)

    def store(z, c, image):
        deeper[z, c] = image
        s = residual[z, c] - step * applied[z, c]
        t = behind[z, c] - step * image
        half[z, c] = s
        response[z, c] = t
        dots[0] += t * s
        dots[1] += t * t
        dots[2] += shadow[z, c] * t
        dots[3] += shadow[z, c] * s

    return coeff_in, coeff_out, store, response, dots


def next_rule(geo, came, packed, inputs, outputs):
    coeff_in, coeff_out, shadow, rho_sums, rho_at, step_in, sums, half, response, applied, deeper, search, moved = inputs
    rho_out, residual_next, behind_next, applied_next, search_next, moved_next = outputs
    smoothing = pick(sums, geo, 0) / pick(sums, geo, 1)
    rho_next = pick(sums, geo, 3) - smoothing * pick(sums, geo, 2)
    step = step_in[0:1, 0:1]
    momentum = (rho_next / rho_sums[0:1, rho_at : rho_at + 1]) * (step / smoothing)
    keep(rho_out, rho_next)
    smoothing, momentum, step = (spread(x, geo.tile) for x in (smoothing, momentum, step))
    dots = zeros(geo, 1)

    def store(z, c, image):
        t = response[z, c]
        s = half[z, c]
        p = search[z, c]
        v = applied[z, c]
        r = s - smoothing * t
        w = t - smoothing * image
        v_next = w + momentum * (v - smoothing * deeper[z, c])
        residual_next[z, c] = r
        behind_next[z, c] = w
        applied_next[z, c] = v_next
        search_next[z, c] = r + momentum * (p - smoothing * v)
        by = step * p + smoothing * s
        moved_next[z, c] = by if moved is None else moved[z, c] + by
        dots[0] += shadow[z, c] * v_next

    return coeff_in, coeff_out, store, applied_next, dots


def last_rule(geo, came, packed, inputs, outputs):
    coeff_out, rho_sums, rho_at, sums, residual, applied, behind, search, moved = inputs
    half, response, moved_next = outputs
    step = spread(rho_sums[0:1, rho_at : rho_at + 1] / pick(sums, geo, 0), geo.tile)
    dots = zeros(geo, 2)

    def store(z, c, image):
        s = residual[z, c] - step * applied[z, c]
        t = behind[z, c] - step * image
        half[z, c] = s
        response[z, c] = t
        by = step * search[z, c]
        moved_next[z, c] = by if moved is None else moved[z, c] + by
        dots[0] += t * s
        dots[1] += t * t

    return None, coeff_out, store, None, dots


def finish_body(geo, came, moved, half, response, guess, inverse, solution_out, residual_out, solution, residual, sems):
    sums = jnp.sum(came[...], axis=0, keepdims=True)
    smoothing = spread(sums[:, 0:1] / sums[:, 1:2], geo.tile)
    copies = []

    def leave(source, target, layer, sem):
        copies.append(pltpu.make_async_copy(source.at[layer], target.at[layer], sem))
        copies[-1].start()

    for z, c in geo.tiles():
        residual[z, c] = half[z, c] - smoothing * response[z, c]
        if c + 1 == geo.comps:
            leave(residual, residual_out, z, sems.at[0, z])

    def put(z, c, block):
        solution[z, c] = guess[z, c] + block
        if z % 2 and c + 1 == geo.comps:
            leave(solution, solution_out, z - 1, sems.at[1, z - 1])
            leave(solution, solution_out, z, sems.at[1, z])

    precondition(geo, inverse, lambda z, c: moved[z, c] + smoothing * half[z, c], put)
    for copy in copies:
        copy.wait()


def exchange(geo, rows):
    wide = rows.reshape(geo.devices, 1, rows.size // geo.devices)
    return lax.all_to_all(wide, AXES, split_axis=0, concat_axis=0, tiled=True).reshape(rows.shape)


def per_device(right_side, guess, diag, mobility, face, inverse, perf_cell, perf_slot, well_in, well_out, well_inverse):
    geo = Geometry(right_side.shape, perf_cell.shape[1:], well_inverse.shape, lax.axis_size("gy"))
    ints = jnp.int32
    block = (geo.devices, LANES)
    packed = (geo.groups_pad, LANES)
    seg = (geo.wells, LANES)
    wide = ((3 * geo.devices, LANES), F32)
    small = ((SUBS, LANES), F32)
    vec = (geo.vector, F32)
    coeffs = ((3,) + packed, F32)
    sent = [vec, (geo.flux, F32), wide]

    table = (perf_cell.shape[1:], ints)
    flux, send, rowp, lanep, spot_hot, hi, lo, inv_dev, inv_pos, inverse_held, guess_held, mobility, well_in, well_out = call(
        functools.partial(first_body, geo),
        [(geo.flux, F32), wide, (packed, ints), (packed, ints), ((2 * LANES, geo.slots), BF16), (block, ints), (block, ints),
         (seg, ints), (seg, ints), (well_inverse.shape, F32), vec, (mobility.shape, BF16), (well_in.shape, F32), (well_out.shape, F32)],
        [], far=[perf_cell[0], perf_slot[0], guess, mobility, well_inverse, well_in, well_out],
        scratch=[pltpu.VMEM(*table), pltpu.VMEM(*table), pltpu.VMEM(block, ints),
                 pltpu.VMEM(packed, ints), pltpu.VMEM((3,) + packed, F32), pltpu.SemaphoreType.DMA((7,))],
    )
    owner_tables = [inv_dev, inv_pos, hi, lo, inverse_held]
    scratch = [pltpu.VMEM(packed, F32), pltpu.VMEM((6 * geo.half_rows, geo.slots), BF16), pltpu.VMEM((3 * geo.tile_rows, LANES), F32)]

    def stage(rule, outs, came, vector, flux, inputs, goes_on=True):
        arrays = [i for i in inputs if i is not None and not isinstance(i, int)]

        def placed(came, packed, refs, out_refs):
            rest = list(refs)
            return rule(geo, came, packed, [i if i is None or isinstance(i, int) else rest.pop(0) for i in inputs], out_refs)

        return call(
            functools.partial(stage_body, geo, placed, len(arrays), len(outs), goes_on),
            outs + (sent if goes_on else [(block, F32)]),
            [came, vector, flux, rowp, lanep, spot_hot] + arrays + [diag, face] + ([inverse, mobility] if goes_on else []), scratch=scratch,
        )

    def owner(send):
        back, sums = call(functools.partial(owner_body, geo), [wide, small], [exchange(geo, send)] + owner_tables)
        return exchange(geo, back), sums

    (back,) = call(
        functools.partial(owner_first_body, geo), [((5 * geo.devices, LANES), F32)], [exchange(geo, send)] + owner_tables + [well_in, well_out]
    )
    shadow, coeff_in, coeff_out, ahead, flux, send = stage(residual_rule, [vec, coeffs, coeffs], exchange(geo, back), guess_held, flux, [right_side])
    always = [coeff_in, coeff_out, shadow]
    came, sums = owner(send)
    rho, rho_at = sums, geo.cap
    applied, ahead, flux, send = stage(image_rule, [vec], came, ahead, flux, always)
    residual, search, behind, moved = shadow, shadow, applied, None
    for iteration in range(ITERS):
        came, sums = owner(send)
        if iteration + 1 == ITERS:
            half, response, moved, send = stage(
                last_rule, [vec] * 3, came, ahead, flux,
                [coeff_out, rho, rho_at, sums, residual, applied, behind, search, moved], goes_on=False,
            )
            break
        step, deeper, half, response, ahead, flux, send = stage(
            half_rule, [small] + [vec] * 3, came, ahead, flux, always + [rho, rho_at, sums, residual, applied, behind]
        )
        came, sums = owner(send)
        rho, residual, behind, applied, search, moved, ahead, flux, send = stage(
            next_rule, [small] + [vec] * 5, came, ahead, flux,
            always + [rho, rho_at, step, sums, half, response, applied, deeper, search, moved],
        )
        rho_at = 0
    return call(
        functools.partial(finish_body, geo), [vec] * 2, [exchange(geo, send), moved, half, response, guess, inverse],
        scratch=[pltpu.VMEM(*vec), pltpu.VMEM(*vec), pltpu.SemaphoreType.DMA((2, geo.layers))], out_far=True,
    )


def solution(mesh):
    in_specs = (
        P(None, None, "gx", "gy"),
        P(None, None, "gx", "gy"),
        P(None, None, None, "gx", "gy"),
        P(None, None, None, "gx", "gy"),
        P(None, None, "gx", "gy"),
        P(None, None, None, "gx", "gy"),
        P(AXES, None, None),
        P(AXES, None, None),
        P(None, AXES),
        P(None, AXES),
        P(AXES, None, None),
    )
    out_specs = (P(None, None, "gx", "gy"), P(None, None, "gx", "gy"))
    return jax.shard_map(per_device, mesh=mesh, in_specs=in_specs, out_specs=out_specs, check_vma=False)
```

```python
import functools

import jax
import jax.numpy as jnp
from jax import lax
from jax.experimental import pallas as pl
from jax.experimental.pallas import tpu as pltpu
from jax.sharding import PartitionSpec as P

ITERS = 2
AXES = ("gx", "gy")
LANES = 128
SUBS = 8
F32 = jnp.float32
BF16 = jnp.bfloat16
SCOPED = 16 * 1024 * 1024


class Geometry:
    def __init__(self, vector_shape, table_shape, inverse_shape, n_gy):
        self.layers, self.comps, self.rows, self.cols = vector_shape
        self.devices, self.cap = table_shape
        self.wells, self.segs = inverse_shape[:2]
        self.n_gy = n_gy
        self.tile_rows = self.layers * self.rows
        self.half_rows = self.tile_rows // 2
        self.faces = self.layers * self.comps
        self.per = LANES // self.cap
        self.groups = -(-self.devices // self.per)
        self.groups_pad = -(-self.groups // SUBS) * SUBS
        self.slots = self.groups * LANES
        self.vector = (self.layers, self.comps, self.rows, self.cols)
        self.flux = (self.faces * self.rows + 2 * SUBS, self.cols)
        self.tile = (self.rows, LANES)
        assert self.cols == LANES and self.segs == LANES and self.rows == 2 * SUBS
        assert self.faces + SUBS <= self.devices and 2 * self.faces <= LANES
        assert 3 * self.cap <= LANES

    def pieces(self):
        for k in range(self.per):
            low = k * self.groups
            count = min(self.groups, self.devices - low)
            if count > 0:
                yield k, low, count

    def tiles(self):
        for z in range(self.layers):
            for c in range(self.comps):
                yield z, c

    def base(self, j):
        return SUBS + j * self.rows


HELD = pl.BlockSpec(memory_space=pltpu.VMEM)
FAR = pl.BlockSpec(memory_space=pltpu.HBM)


def call(body, outs, args, far=(), scratch=(), out_far=False):
    held = [pltpu.with_memory_space_constraint(a, pltpu.VMEM) for a in args]
    far = [pltpu.with_memory_space_constraint(a, pltpu.HBM) for a in far]
    shapes = [jax.ShapeDtypeStruct(*o) if out_far else pltpu.VMEM(*o) for o in outs]
    return pl.pallas_call(
        body,
        out_shape=tuple(shapes),
        in_specs=[HELD] * len(held) + [FAR] * len(far),
        out_specs=(FAR if out_far else HELD,) * len(outs),
        scratch_shapes=list(scratch),
        compiler_params=pltpu.CompilerParams(vmem_limit_bytes=SCOPED),
    )(*held, *far)


class Rows:
    def __init__(self, ref, width):
        self.ref, self.width = ref, width
        self.devices = ref.shape[0] // width

    def at(self, k, low=0, count=None):
        count = self.devices - low if count is None else count
        start = low * self.width + k
        if self.width == 1 or count == 1:
            return (slice(start, start + count), slice(None))
        return (pl.ds(start, count, stride=self.width), slice(None))

    def get(self, k, low=0, count=None):
        return self.ref[self.at(k, low, count)]

    def put(self, k, value, low=0):
        self.ref[self.at(k, low, value.shape[0])] = value


def iota(shape, dim):
    return lax.broadcasted_iota(jnp.int32, shape, dim)


def take_lanes(table, index):
    return jnp.take_along_axis(table, index, axis=1, mode="promise_in_bounds")


def spread(row, shape):
    return jnp.broadcast_to(row, shape)


def total(block):
    return jnp.sum(jnp.sum(block, axis=0, keepdims=True), axis=1, keepdims=True)


def one_hot(index, size):
    rows = spread(index, (size, LANES))
    return jnp.where(rows == iota(rows.shape, 0), 1.0, 0.0).astype(BF16)


def pack_slots(geo, rows, at_row, lane, packed_ref):
    packed_ref[...] = jnp.zeros_like(packed_ref)
    for k, low, count in geo.pieces():
        part = rows.get(at_row, low, count)
        shift = (k * geo.cap - lane) % LANES
        part = pltpu.roll(part, shift, 1) if shift else part
        at = iota(part.shape, 1)
        mine = (at >= k * geo.cap) & (at < (k + 1) * geo.cap)
        packed_ref[0:count, :] = jnp.where(mine, part, packed_ref[0:count, :])


def unpack_slots(geo, packed, lane, rows):
    for k, low, count in geo.pieces():
        shift = (lane - k * geo.cap) % LANES
        part = pltpu.roll(packed, shift, 1) if shift else packed
        part = part[0:count]
        at = iota(part.shape, 1)
        mine = (at >= lane) & (at < lane + geo.cap)
        rows.put(0, jnp.where(mine, part, rows.get(0, low, count)), low)


def write_faces(geo, flux, send):
    if geo.devices > geo.faces + SUBS:
        nothing = jnp.zeros((geo.devices - geo.faces - SUBS, LANES), F32)
        send.put(1, nothing, geo.faces + SUBS)
        send.put(2, nothing, geo.faces + SUBS)
    send.put(1, flux[pl.ds(geo.base(0), geo.faces, stride=geo.rows), :])
    send.put(2, flux[pl.ds(geo.base(0) + geo.rows - 1, geo.faces, stride=geo.rows), :])
    at = iota(geo.tile, 1) >> 1
    edges = jnp.zeros(geo.tile, F32)
    for j in range(geo.faces):
        turned = pltpu.roll(flux[geo.base(j) : geo.base(j) + geo.rows, :], 2 * j + 1, 1)
        edges = jnp.where(at == j, turned, edges)
    send.put(1, edges[:SUBS], geo.faces)
    send.put(2, edges[SUBS:], geo.faces)


def write_flux(geo, mobility, vector, flux):
    flux[0:SUBS, :] = jnp.zeros((SUBS, LANES), F32)
    flux[geo.base(geo.faces) :, :] = jnp.zeros((SUBS, LANES), F32)
    for z in range(geo.layers):
        v = [vector[z, b] for b in range(3)]
        for a in range(3):
            block = mobility[z, a, 0].astype(F32) * v[0]
            block += mobility[z, a, 1].astype(F32) * v[1]
            block += mobility[z, a, 2].astype(F32) * v[2]
            base = geo.base(3 * z + a)
            flux[base : base + geo.rows, :] = block


def gather_cells(geo, vector, rowp, lanep, finish):
    shape = (SUBS, LANES)
    for g in range(geo.groups):
        lane = spread(lanep[g : g + 1, :], shape)
        row = spread(rowp[g : g + 1, :], shape) - iota(shape, 0)
        kept = [jnp.zeros(shape, F32) for _ in range(3)]
        for z in range(geo.layers):
            for h in range(geo.rows // SUBS):
                mine = row == z * geo.rows + h * SUBS
                for c in range(3):
                    found = take_lanes(vector[z, c, h * SUBS : (h + 1) * SUBS, :], lane)
                    kept[c] = jnp.where(mine, found, kept[c])
        finish(g, kept)


def precondition(geo, inverse, source, target):
    for h in range(geo.layers // 2):
        v = [source(2 * h + f // 3, f % 3) for f in range(6)]
        for e in range(6):
            block = inverse[h, e, 0].astype(F32) * v[0]
            for f in range(1, 6):
                block += inverse[h, e, f].astype(F32) * v[f]
            target(2 * h + e // 3, e % 3, block)


def first_body(geo, *refs):
    far, refs = refs[:7], refs[7:]
    (flux, send, rowp, lanep, spot_hot, hi, lo, inv_dev, inv_pos, inverse_held, guess, mobility, well_in, well_out), refs = refs[:14], refs[14:]
    cells, slots, wide, ints, packed, sems = refs
    send = Rows(send, 3)
    targets = (cells, slots, guess, mobility, inverse_held, well_in, well_out)
    copies = [pltpu.make_async_copy(source, target, sems.at[i]) for i, (source, target) in enumerate(zip(far, targets))]
    for i in (0, 2, 3, 1, 4, 5, 6):
        copies[i].start()
    wide[...] = jnp.zeros_like(wide)
    copies[0].wait()
    wide[:, 0 : geo.cap] = cells[...] + 1
    pack_slots(geo, Rows(wide, 1), 0, 0, ints)
    index = ints[...] - 1
    rowp[...] = index >> 7
    lanep[...] = index & (LANES - 1)
    copies[1].wait()
    slot_tables(geo, slots, hi, lo, inv_dev, inv_pos, wide, ints)
    for g in range(geo.groups):
        row, lane = rowp[g : g + 1, :], lanep[g : g + 1, :]
        upper = jnp.where(row >= geo.half_rows, LANES, 0)
        spot_hot[:, g * LANES : (g + 1) * LANES] = one_hot(upper + lane, 2 * LANES)
    copies[2].wait()
    copies[3].wait()
    write_flux(geo, mobility, guess, flux)
    write_faces(geo, flux, send)
    send.put(0, jnp.zeros((geo.devices, LANES), F32))
    packed[...] = jnp.zeros_like(packed)

    def finish(g, kept):
        for c in range(3):
            packed[c, g : g + 1, :] = jnp.sum(kept[c], axis=0, keepdims=True)

    gather_cells(geo, guess, rowp, lanep, finish)
    for c in range(3):
        unpack_slots(geo, packed[c], c * geo.cap, send)
    for copy in copies[4:]:
        copy.wait()


def slot_tables(geo, slot_ref, hi, lo, inv_dev, inv_pos, wide, packed):
    wide[:, 0 : geo.cap] = slot_ref[...] + 1
    slots = wide[...] - 1
    hi[...] = slots >> 7
    lo[...] = slots & (LANES - 1)
    pack_slots(geo, Rows(wide, 1), 0, 0, packed)
    slots = packed[...] - 1
    slot_hi = slots >> 7
    slot_lo = slots & (LANES - 1)
    at = iota((geo.wells, LANES), 1)
    piece = lax.div(at, geo.cap)
    position = (lax.rem(at, geo.cap) + 1).astype(F32)
    found = jnp.zeros((2 * geo.wells, LANES), F32)
    for g in range(geo.groups):
        well = spread(slot_hi[g : g + 1], (geo.wells, LANES)) == iota((geo.wells, LANES), 0)
        device = (piece * geo.groups + (g + 1)).astype(F32)
        marks = jnp.concatenate([jnp.where(well, device, 0.0), jnp.where(well, position, 0.0)], axis=0)
        hot = one_hot(slot_lo[g : g + 1], LANES)
        found += lax.dot_general(marks.astype(BF16), hot, (((1,), (1,)), ((), ())), preferred_element_type=F32)
    inv_dev[...] = found[: geo.wells].astype(jnp.int32) - 1
    inv_pos[...] = jnp.maximum(found[geo.wells :].astype(jnp.int32) - 1, 0)


def relay(geo, came, back):
    shape = (geo.devices, LANES)
    at = iota(shape, 0)
    even = (iota(shape, 1) & 1) == 0
    within = lax.rem(at, geo.n_gy)
    faces = jnp.full(shape, lax.axis_index(AXES), jnp.int32) < geo.faces
    up, down, count = geo.n_gy, geo.devices - geo.n_gy, geo.devices
    one, two = came.get(1), came.get(2)
    after = jnp.where(at < down, pltpu.roll(one, down, 0), 0.0)
    before = jnp.where(at >= up, pltpu.roll(two, up, 0), 0.0)

    def beside(block):
        low = jnp.where(within > 0, pltpu.roll(pltpu.roll(block, 1, 1), 1, 0), 0.0)
        high = jnp.where(within < geo.n_gy - 1, pltpu.roll(pltpu.roll(block, LANES - 1, 1), count - 1, 0), 0.0)
        return jnp.where(even, high, low)

    back.put(1, jnp.where(faces, after, beside(one)))
    back.put(2, jnp.where(faces, before, beside(two)))


def at_segments(geo, came, inv_dev, inv_pos, offset):
    shape = (geo.wells, LANES)
    device = inv_dev[...]
    position = inv_pos[...] + offset
    kept = jnp.zeros(shape, F32)
    for s in range(geo.devices):
        found = take_lanes(spread(came.get(0, s, 1), shape), position)
        kept = jnp.where(device == s, found, kept)
    return kept


def at_slots(geo, rows, hi, lo):
    shape = (geo.devices, LANES)
    kept = jnp.zeros(shape, F32)
    for w in range(geo.wells):
        found = take_lanes(spread(rows[w], shape), lo)
        kept = jnp.where(hi == w, found, kept)
    return kept


def solve_segments(geo, rate, inverse):
    shape = (geo.segs, LANES)
    own = iota(shape, 0) == iota(shape, 1)
    rows = []
    for w in range(geo.wells):
        sums = jnp.sum(inverse[w] * rate[w : w + 1, :], axis=1, keepdims=True)
        rows.append(jnp.sum(jnp.where(own, spread(sums, shape), 0.0), axis=0, keepdims=True))
    return rows


def owner_first_body(geo, came, inv_dev, inv_pos, hi_ref, lo_ref, inverse_held, well_in, well_out, back):
    came, back = Rows(came, 3), Rows(back, 5)
    hi, lo = hi_ref[...], lo_ref[...]
    rows_in = [[well_in[c : c + 1, w * LANES : (w + 1) * LANES] for w in range(geo.wells)] for c in range(3)]
    rows_out = [[well_out[c : c + 1, w * LANES : (w + 1) * LANES] for w in range(geo.wells)] for c in range(3)]
    rate = jnp.zeros((geo.wells, LANES), F32)
    for c in range(3):
        rate += jnp.concatenate(rows_in[c], axis=0) * at_segments(geo, came, inv_dev, inv_pos, c * geo.cap)
    back.put(0, at_slots(geo, solve_segments(geo, rate, inverse_held), hi, lo))
    relay(geo, came, back)
    for place, rows in ((3, rows_in), (4, rows_out)):
        block = jnp.zeros((geo.devices, LANES), F32)
        for c in range(3):
            part = at_slots(geo, rows[c], hi, lo)
            block += pltpu.roll(part, c * geo.cap, 1) if c else part
        back.put(place, block)


def owner_body(geo, came, inv_dev, inv_pos, hi_ref, lo_ref, inverse_held, back, sums):
    came, back = Rows(came, 3), Rows(back, 3)
    rate = at_segments(geo, came, inv_dev, inv_pos, 0)
    back.put(0, at_slots(geo, solve_segments(geo, rate, inverse_held), hi_ref[...], lo_ref[...]))
    relay(geo, came, back)
    sums[...] = spread(jnp.sum(came.get(0), axis=0, keepdims=True), sums.shape)


def scatter_terms(geo, came, coeff_out, rowp, spot_hot, packed, left, spots):
    pack_slots(geo, came, 0, 0, packed)
    rate = packed[...]
    parts = []
    for c in range(3):
        value = coeff_out[c] * rate
        high = value.astype(BF16)
        parts += [high, (value - high.astype(F32)).astype(BF16)]
    n = geo.half_rows
    row = rowp[...]
    row = jnp.where(row >= n, row - n, row)
    for g in range(geo.groups):
        hot = one_hot(row[g : g + 1], n)
        for i, part in enumerate(parts):
            left[i * n : (i + 1) * n, g * LANES : (g + 1) * LANES] = hot * spread(part[g : g + 1], hot.shape)
    result = lax.dot_general(left[...], spot_hot[...], (((1,), (1,)), ((), ())), preferred_element_type=F32)
    for c in range(3):
        i = 2 * c * n
        summed = result[i : i + n] + result[i + n : i + 2 * n]
        for h in range(2):
            low = c * geo.tile_rows + h * n
            spots[low : low + n, :] = summed[:, h * LANES : (h + 1) * LANES]


def apply_operator(geo, came, vector, flux, diag, face, spots, store):
    at_row, at_lane = iota((SUBS, LANES), 0), iota(geo.tile, 1)
    edges = jnp.concatenate([came.get(1, geo.faces, SUBS), came.get(2, geo.faces, SUBS)], axis=0)
    for z in range(geo.layers):
        f = [face[n, z].astype(F32) for n in range(6)]
        v = [vector[z, b] for b in range(3)]
        for a in range(3):
            j = 3 * z + a
            base = geo.base(j)
            block = flux[base : base + geo.rows, :]
            first = jnp.where(at_row == 0, spread(came.get(2, j, 1), at_row.shape), flux[base - 1 : base - 1 + SUBS, :])
            under = jnp.concatenate([first, flux[base - 1 + SUBS : base - 1 + geo.rows, :]], axis=0)
            final = jnp.where(at_row == SUBS - 1, spread(came.get(1, j, 1), at_row.shape), flux[base + 1 + SUBS : base + 1 + geo.rows, :])
            over = jnp.concatenate([flux[base + 1 : base + 1 + SUBS, :], final], axis=0)
            ends = pltpu.roll(edges, LANES - 1 - 2 * j, 1)
            left = jnp.where(at_lane == 0, ends, pltpu.roll(block, 1, 1))
            right = jnp.where(at_lane == LANES - 1, ends, pltpu.roll(block, LANES - 1, 1))
            beside = f[0] * under + f[1] * over + f[2] * left + f[3] * right
            if z > 0:
                beside += f[4] * flux[base - 3 * geo.rows : base - 2 * geo.rows, :]
            if z + 1 < geo.layers:
                beside += f[5] * flux[base + 3 * geo.rows : base + 4 * geo.rows, :]
            own = diag[z, a, 0].astype(F32) * v[0]
            own += diag[z, a, 1].astype(F32) * v[1]
            own += diag[z, a, 2].astype(F32) * v[2]
            low = a * geo.tile_rows + z * geo.rows
            store(z, a, own - beside - spots[low : low + geo.rows, :])


def send_next(geo, source, inverse, mobility, rowp, lanep, coeff_in, dots, ahead, flux, send, packed):
    def put(z, c, block):
        ahead[z, c] = block

    precondition(geo, inverse, lambda z, c: source[z, c], put)
    at = iota((1, LANES), 1)
    row = jnp.zeros((1, LANES), F32)
    for n, dot in enumerate(dots):
        row = jnp.where(at == geo.cap + n, spread(total(dot), (1, LANES)), row)
    send.put(0, spread(row, (geo.devices, LANES)))
    packed[...] = jnp.zeros_like(packed)

    def finish(g, kept):
        rate = kept[0] * spread(coeff_in[0, g : g + 1, :], kept[0].shape)
        rate += kept[1] * spread(coeff_in[1, g : g + 1, :], kept[0].shape)
        rate += kept[2] * spread(coeff_in[2, g : g + 1, :], kept[0].shape)
        packed[g : g + 1, :] = jnp.sum(rate, axis=0, keepdims=True)

    gather_cells(geo, ahead, rowp, lanep, finish)
    write_flux(geo, mobility, ahead, flux)
    write_faces(geo, flux, send)
    unpack_slots(geo, packed[...], 0, send)


def stage_body(geo, rule, n_in, n_out, goes_on, *refs):
    refs = list(refs)

    def take(n):
        got, refs[:n] = refs[:n], []
        return got

    came, vector, flux_in, rowp, lanep, spot_hot = take(6)
    inputs = take(n_in)
    diag, face, *hats = take(4 if goes_on else 2)
    outputs = take(n_out)
    following = take(3) if goes_on else take(1)
    packed, left, spots = take(3)
    came = Rows(came, came.shape[0] // geo.devices)
    coeff_in, coeff_out, store, source, dots = rule(came, packed, inputs, outputs)
    scatter_terms(geo, came, coeff_out, rowp, spot_hot, packed, left, spots)
    apply_operator(geo, came, vector, flux_in, diag, face, spots, store)
    if goes_on:
        ahead, flux, send = following
        send = Rows(send, 3)
        send_next(geo, source, *hats, rowp, lanep, coeff_in, dots, ahead, flux, send, packed)
    else:
        at = iota((1, LANES), 1)
        row = jnp.where(at == 0, spread(total(dots[0]), (1, LANES)), spread(total(dots[1]), (1, LANES)))
        following[0][...] = spread(row, following[0].shape)


def zeros(geo, count):
    return [jnp.zeros(geo.tile, F32) for _ in range(count)]


def pick(sums, geo, n):
    return sums[0:1, geo.cap + n : geo.cap + n + 1]


def keep(ref, value):
    ref[...] = spread(value, ref.shape)


def residual_rule(geo, came, packed, inputs, outputs):
    (right_side,) = inputs
    shadow, coeff_in, coeff_out = outputs
    for c in range(3):
        pack_slots(geo, came, 3, c * geo.cap, packed)
        coeff_in[c] = packed[...]
        pack_slots(geo, came, 4, c * geo.cap, packed)
        coeff_out[c] = packed[...]
    dots = zeros(geo, 1)

    def store(z, c, image):
        value = right_side[z, c] - image
        shadow[z, c] = value
        dots[0] += value * value

    return coeff_in, coeff_out, store, shadow, dots


def image_rule(geo, came, packed, inputs, outputs):
    coeff_in, coeff_out, shadow = inputs
    (applied,) = outputs
    dots = zeros(geo, 1)

    def store(z, c, image):
        applied[z, c] = image
        dots[0] += shadow[z, c] * image

    return coeff_in, coeff_out, store, applied, dots


def half_rule(geo, came, packed, inputs, outputs):
    coeff_in, coeff_out, shadow, rho_sums, rho_at, sums, residual, applied, behind = inputs
    step_out, deeper, half, response = outputs
    step = rho_sums[0:1, rho_at : rho_at + 1] / pick(sums, geo, 0)
    keep(step_out, step)
    step = spread(step, geo.tile)
    dots = zeros(geo, 4)

    def store(z, c, image):
        deeper[z, c] = image
        s = residual[z, c] - step * applied[z, c]
        t = behind[z, c] - step * image
        half[z, c] = s
        response[z, c] = t
        dots[0] += t * s
        dots[1] += t * t
        dots[2] += shadow[z, c] * t
        dots[3] += shadow[z, c] * s

    return coeff_in, coeff_out, store, response, dots


def next_rule(geo, came, packed, inputs, outputs):
    coeff_in, coeff_out, shadow, rho_sums, rho_at, step_in, sums, half, response, applied, deeper, search, moved = inputs
    rho_out, residual_next, behind_next, applied_next, search_next, moved_next = outputs
    smoothing = pick(sums, geo, 0) / pick(sums, geo, 1)
    rho_next = pick(sums, geo, 3) - smoothing * pick(sums, geo, 2)
    step = step_in[0:1, 0:1]
    momentum = (rho_next / rho_sums[0:1, rho_at : rho_at + 1]) * (step / smoothing)
    keep(rho_out, rho_next)
    smoothing, momentum, step = (spread(x, geo.tile) for x in (smoothing, momentum, step))
    dots = zeros(geo, 1)

    def store(z, c, image):
        t = response[z, c]
        s = half[z, c]
        p = search[z, c]
        v = applied[z, c]
        r = s - smoothing * t
        w = t - smoothing * image
        v_next = w + momentum * (v - smoothing * deeper[z, c])
        residual_next[z, c] = r
        behind_next[z, c] = w
        applied_next[z, c] = v_next
        search_next[z, c] = r + momentum * (p - smoothing * v)
        by = step * p + smoothing * s
        moved_next[z, c] = by if moved is None else moved[z, c] + by
        dots[0] += shadow[z, c] * v_next

    return coeff_in, coeff_out, store, applied_next, dots


def last_rule(geo, came, packed, inputs, outputs):
    coeff_out, rho_sums, rho_at, sums, residual, applied, behind, search, moved = inputs
    half, response, moved_next = outputs
    step = spread(rho_sums[0:1, rho_at : rho_at + 1] / pick(sums, geo, 0), geo.tile)
    dots = zeros(geo, 2)

    def store(z, c, image):
        s = residual[z, c] - step * applied[z, c]
        t = behind[z, c] - step * image
        half[z, c] = s
        response[z, c] = t
        by = step * search[z, c]
        moved_next[z, c] = by if moved is None else moved[z, c] + by
        dots[0] += t * s
        dots[1] += t * t

    return None, coeff_out, store, None, dots


def finish_body(geo, came, moved, half, response, guess, inverse, solution_out, residual_out, solution, residual, sems):
    sums = jnp.sum(came[...], axis=0, keepdims=True)
    smoothing = spread(sums[:, 0:1] / sums[:, 1:2], geo.tile)
    copies = []

    def leave(source, target, layer, sem):
        copies.append(pltpu.make_async_copy(source.at[layer], target.at[layer], sem))
        copies[-1].start()

    for z, c in geo.tiles():
        residual[z, c] = half[z, c] - smoothing * response[z, c]
        if c + 1 == geo.comps:
            leave(residual, residual_out, z, sems.at[0, z])

    def put(z, c, block):
        solution[z, c] = guess[z, c] + block
        if z % 2 and c + 1 == geo.comps:
            leave(solution, solution_out, z - 1, sems.at[1, z - 1])
            leave(solution, solution_out, z, sems.at[1, z])

    precondition(geo, inverse, lambda z, c: moved[z, c] + smoothing * half[z, c], put)
    for copy in copies:
        copy.wait()


def exchange(geo, rows):
    wide = rows.reshape(geo.devices, 1, rows.size // geo.devices)
    return lax.all_to_all(wide, AXES, split_axis=0, concat_axis=0, tiled=True).reshape(rows.shape)


def per_device(right_side, guess, diag, mobility, face, inverse, perf_cell, perf_slot, well_in, well_out, well_inverse):
    geo = Geometry(right_side.shape, perf_cell.shape[1:], well_inverse.shape, lax.axis_size("gy"))
    ints = jnp.int32
    block = (geo.devices, LANES)
    packed = (geo.groups_pad, LANES)
    seg = (geo.wells, LANES)
    wide = ((3 * geo.devices, LANES), F32)
    small = ((SUBS, LANES), F32)
    vec = (geo.vector, F32)
    coeffs = ((3,) + packed, F32)
    sent = [vec, (geo.flux, F32), wide]

    table = (perf_cell.shape[1:], ints)
    flux, send, rowp, lanep, spot_hot, hi, lo, inv_dev, inv_pos, inverse_held, guess_held, mobility, well_in, well_out = call(
        functools.partial(first_body, geo),
        [(geo.flux, F32), wide, (packed, ints), (packed, ints), ((2 * LANES, geo.slots), BF16), (block, ints), (block, ints),
         (seg, ints), (seg, ints), (well_inverse.shape, F32), vec, (mobility.shape, BF16), (well_in.shape, F32), (well_out.shape, F32)],
        [], far=[perf_cell[0], perf_slot[0], guess, mobility, well_inverse, well_in, well_out],
        scratch=[pltpu.VMEM(*table), pltpu.VMEM(*table), pltpu.VMEM(block, ints),
                 pltpu.VMEM(packed, ints), pltpu.VMEM((3,) + packed, F32), pltpu.SemaphoreType.DMA((7,))],
    )
    owner_tables = [inv_dev, inv_pos, hi, lo, inverse_held]
    scratch = [pltpu.VMEM(packed, F32), pltpu.VMEM((6 * geo.half_rows, geo.slots), BF16), pltpu.VMEM((3 * geo.tile_rows, LANES), F32)]

    def stage(rule, outs, came, vector, flux, inputs, goes_on=True):
        arrays = [i for i in inputs if i is not None and not isinstance(i, int)]

        def placed(came, packed, refs, out_refs):
            rest = list(refs)
            return rule(geo, came, packed, [i if i is None or isinstance(i, int) else rest.pop(0) for i in inputs], out_refs)

        return call(
            functools.partial(stage_body, geo, placed, len(arrays), len(outs), goes_on),
            outs + (sent if goes_on else [(block, F32)]),
            [came, vector, flux, rowp, lanep, spot_hot] + arrays + [diag, face] + ([inverse, mobility] if goes_on else []), scratch=scratch,
        )

    def owner(send):
        back, sums = call(functools.partial(owner_body, geo), [wide, small], [exchange(geo, send)] + owner_tables)
        return exchange(geo, back), sums

    (back,) = call(
        functools.partial(owner_first_body, geo), [((5 * geo.devices, LANES), F32)], [exchange(geo, send)] + owner_tables + [well_in, well_out]
    )
    shadow, coeff_in, coeff_out, ahead, flux, send = stage(residual_rule, [vec, coeffs, coeffs], exchange(geo, back), guess_held, flux, [right_side])
    always = [coeff_in, coeff_out, shadow]
    came, sums = owner(send)
    rho, rho_at = sums, geo.cap
    applied, ahead, flux, send = stage(image_rule, [vec], came, ahead, flux, always)
    residual, search, behind, moved = shadow, shadow, applied, None
    for iteration in range(ITERS):
        came, sums = owner(send)
        if iteration + 1 == ITERS:
            half, response, moved, send = stage(
                last_rule, [vec] * 3, came, ahead, flux,
                [coeff_out, rho, rho_at, sums, residual, applied, behind, search, moved], goes_on=False,
            )
            break
        step, deeper, half, response, ahead, flux, send = stage(
            half_rule, [small] + [vec] * 3, came, ahead, flux, always + [rho, rho_at, sums, residual, applied, behind]
        )
        came, sums = owner(send)
        rho, residual, behind, applied, search, moved, ahead, flux, send = stage(
            next_rule, [small] + [vec] * 5, came, ahead, flux,
            always + [rho, rho_at, step, sums, half, response, applied, deeper, search, moved],
        )
        rho_at = 0
    return call(
        functools.partial(finish_body, geo), [vec] * 2, [exchange(geo, send), moved, half, response, guess, inverse],
        scratch=[pltpu.VMEM(*vec), pltpu.VMEM(*vec), pltpu.SemaphoreType.DMA((2, geo.layers))], out_far=True,
    )


def solution(mesh):
    in_specs = (
        P(None, None, "gx", "gy"),
        P(None, None, "gx", "gy"),
        P(None, None, None, "gx", "gy"),
        P(None, None, None, "gx", "gy"),
        P(None, None, "gx", "gy"),
        P(None, None, None, "gx", "gy"),
        P(AXES, None, None),
        P(AXES, None, None),
        P(None, AXES),
        P(None, AXES),
        P(AXES, None, None),
    )
    out_specs = (P(None, None, "gx", "gy"), P(None, None, "gx", "gy"))
    return jax.shard_map(per_device, mesh=mesh, in_specs=in_specs, out_specs=out_specs, check_vma=False)
```

```python
import functools

import jax
import jax.numpy as jnp
from jax import lax
from jax.experimental import pallas as pl
from jax.experimental.pallas import tpu as pltpu
from jax.sharding import PartitionSpec as P

ITERS = 2
AXES = ("gx", "gy")
LANES = 128
SUBS = 8
F32 = jnp.float32
BF16 = jnp.bfloat16
SCOPED = 16 * 1024 * 1024


class Geometry:
    def __init__(self, vector_shape, table_shape, inverse_shape, n_gy):
        self.layers, self.comps, self.rows, self.cols = vector_shape
        self.devices, self.cap = table_shape
        self.wells, self.segs = inverse_shape[:2]
        self.n_gy = n_gy
        self.tile_rows = self.layers * self.rows
        self.half_rows = self.tile_rows // 2
        self.faces = self.layers * self.comps
        self.per = LANES // self.cap
        self.groups = -(-self.devices // self.per)
        self.groups_pad = -(-self.groups // SUBS) * SUBS
        self.slots = self.groups * LANES
        self.vector = (self.layers, self.comps, self.rows, self.cols)
        self.flux = (self.faces * self.rows + 2 * SUBS, self.cols)
        self.tile = (self.rows, LANES)
        assert self.cols == LANES and self.segs == LANES and self.rows == 2 * SUBS
        assert self.faces + SUBS <= self.devices and 2 * self.faces <= LANES
        assert 3 * self.cap <= LANES

    def pieces(self):
        for k in range(self.per):
            low = k * self.groups
            count = min(self.groups, self.devices - low)
            if count > 0:
                yield k, low, count

    def tiles(self):
        for z in range(self.layers):
            for c in range(self.comps):
                yield z, c

    def base(self, j):
        return SUBS + j * self.rows


HELD = pl.BlockSpec(memory_space=pltpu.VMEM)
FAR = pl.BlockSpec(memory_space=pltpu.HBM)


def call(body, outs, args, far=(), scratch=(), out_far=False):
    held = [pltpu.with_memory_space_constraint(a, pltpu.VMEM) for a in args]
    far = [pltpu.with_memory_space_constraint(a, pltpu.HBM) for a in far]
    shapes = [jax.ShapeDtypeStruct(*o) if out_far else pltpu.VMEM(*o) for o in outs]
    return pl.pallas_call(
        body,
        out_shape=tuple(shapes),
        in_specs=[HELD] * len(held) + [FAR] * len(far),
        out_specs=(FAR if out_far else HELD,) * len(outs),
        scratch_shapes=list(scratch),
        compiler_params=pltpu.CompilerParams(vmem_limit_bytes=SCOPED),
    )(*held, *far)


class Rows:
    def __init__(self, ref, width):
        self.ref, self.width = ref, width
        self.devices = ref.shape[0] // width

    def at(self, k, low=0, count=None):
        count = self.devices - low if count is None else count
        start = low * self.width + k
        if self.width == 1 or count == 1:
            return (slice(start, start + count), slice(None))
        return (pl.ds(start, count, stride=self.width), slice(None))

    def get(self, k, low=0, count=None):
        return self.ref[self.at(k, low, count)]

    def put(self, k, value, low=0):
        self.ref[self.at(k, low, value.shape[0])] = value


def iota(shape, dim):
    return lax.broadcasted_iota(jnp.int32, shape, dim)


def take_lanes(table, index):
    return jnp.take_along_axis(table, index, axis=1, mode="promise_in_bounds")


def spread(row, shape):
    return jnp.broadcast_to(row, shape)


def total(block):
    return jnp.sum(jnp.sum(block, axis=0, keepdims=True), axis=1, keepdims=True)


def one_hot(index, size):
    rows = spread(index, (size, LANES))
    return jnp.where(rows == iota(rows.shape, 0), 1.0, 0.0).astype(BF16)


def pack_slots(geo, rows, at_row, lane, packed_ref):
    packed_ref[...] = jnp.zeros_like(packed_ref)
    for k, low, count in geo.pieces():
        part = rows.get(at_row, low, count)
        shift = (k * geo.cap - lane) % LANES
        part = pltpu.roll(part, shift, 1) if shift else part
        at = iota(part.shape, 1)
        mine = (at >= k * geo.cap) & (at < (k + 1) * geo.cap)
        packed_ref[0:count, :] = jnp.where(mine, part, packed_ref[0:count, :])


def unpack_slots(geo, packed, lane, rows):
    for k, low, count in geo.pieces():
        shift = (lane - k * geo.cap) % LANES
        part = pltpu.roll(packed, shift, 1) if shift else packed
        part = part[0:count]
        at = iota(part.shape, 1)
        mine = (at >= lane) & (at < lane + geo.cap)
        rows.put(0, jnp.where(mine, part, rows.get(0, low, count)), low)


def write_faces(geo, flux, send):
    if geo.devices > geo.faces + SUBS:
        nothing = jnp.zeros((geo.devices - geo.faces - SUBS, LANES), F32)
        send.put(1, nothing, geo.faces + SUBS)
        send.put(2, nothing, geo.faces + SUBS)
    send.put(1, flux[pl.ds(geo.base(0), geo.faces, stride=geo.rows), :])
    send.put(2, flux[pl.ds(geo.base(0) + geo.rows - 1, geo.faces, stride=geo.rows), :])
    at = iota(geo.tile, 1) >> 1
    edges = jnp.zeros(geo.tile, F32)
    for j in range(geo.faces):
        turned = pltpu.roll(flux[geo.base(j) : geo.base(j) + geo.rows, :], 2 * j + 1, 1)
        edges = jnp.where(at == j, turned, edges)
    send.put(1, edges[:SUBS], geo.faces)
    send.put(2, edges[SUBS:], geo.faces)


def write_flux(geo, mobility, vector, flux):
    flux[0:SUBS, :] = jnp.zeros((SUBS, LANES), F32)
    flux[geo.base(geo.faces) :, :] = jnp.zeros((SUBS, LANES), F32)
    for z in range(geo.layers):
        v = [vector[z, b] for b in range(3)]
        for a in range(3):
            block = mobility[z, a, 0].astype(F32) * v[0]
            block += mobility[z, a, 1].astype(F32) * v[1]
            block += mobility[z, a, 2].astype(F32) * v[2]
            base = geo.base(3 * z + a)
            flux[base : base + geo.rows, :] = block


def gather_cells(geo, vector, rowp, lanep, finish):
    shape = (SUBS, LANES)
    for g in range(geo.groups):
        lane = spread(lanep[g : g + 1, :], shape)
        row = spread(rowp[g : g + 1, :], shape) - iota(shape, 0)
        kept = [jnp.zeros(shape, F32) for _ in range(3)]
        for z in range(geo.layers):
            for h in range(geo.rows // SUBS):
                mine = row == z * geo.rows + h * SUBS
                for c in range(3):
                    found = take_lanes(vector[z, c, h * SUBS : (h + 1) * SUBS, :], lane)
                    kept[c] = jnp.where(mine, found, kept[c])
        finish(g, kept)


def precondition(geo, inverse, source, target):
    for h in range(geo.layers // 2):
        v = [source(2 * h + f // 3, f % 3) for f in range(6)]
        for e in range(6):
            block = inverse[h, e, 0].astype(F32) * v[0]
            for f in range(1, 6):
                block += inverse[h, e, f].astype(F32) * v[f]
            target(2 * h + e // 3, e % 3, block)


def first_body(geo, *refs):
    far, refs = refs[:7], refs[7:]
    (flux, send, rowp, lanep, spot_hot, hi, lo, inv_dev, inv_pos, inverse_held, guess, mobility, well_in, well_out), refs = refs[:14], refs[14:]
    cells, slots, wide, ints, packed, sems = refs
    send = Rows(send, 3)
    targets = (cells, slots, guess, mobility, inverse_held, well_in, well_out)
    copies = [pltpu.make_async_copy(source, target, sems.at[i]) for i, (source, target) in enumerate(zip(far, targets))]
    for i in (0, 2, 3, 1, 4, 5, 6):
        copies[i].start()
    wide[...] = jnp.zeros_like(wide)
    copies[0].wait()
    wide[:, 0 : geo.cap] = cells[...] + 1
    pack_slots(geo, Rows(wide, 1), 0, 0, ints)
    index = ints[...] - 1
    rowp[...] = index >> 7
    lanep[...] = index & (LANES - 1)
    copies[1].wait()
    slot_tables(geo, slots, hi, lo, inv_dev, inv_pos, wide, ints)
    for g in range(geo.groups):
        row, lane = rowp[g : g + 1, :], lanep[g : g + 1, :]
        upper = jnp.where(row >= geo.half_rows, LANES, 0)
        spot_hot[:, g * LANES : (g + 1) * LANES] = one_hot(upper + lane, 2 * LANES)
    copies[2].wait()
    copies[3].wait()
    write_flux(geo, mobility, guess, flux)
    write_faces(geo, flux, send)
    send.put(0, jnp.zeros((geo.devices, LANES), F32))
    packed[...] = jnp.zeros_like(packed)

    def finish(g, kept):
        for c in range(3):
            packed[c, g : g + 1, :] = jnp.sum(kept[c], axis=0, keepdims=True)

    gather_cells(geo, guess, rowp, lanep, finish)
    for c in range(3):
        unpack_slots(geo, packed[c], c * geo.cap, send)
    for copy in copies[4:]:
        copy.wait()


def slot_tables(geo, slot_ref, hi, lo, inv_dev, inv_pos, wide, packed):
    wide[:, 0 : geo.cap] = slot_ref[...] + 1
    slots = wide[...] - 1
    hi[...] = slots >> 7
    lo[...] = slots & (LANES - 1)
    pack_slots(geo, Rows(wide, 1), 0, 0, packed)
    slots = packed[...] - 1
    slot_hi = slots >> 7
    slot_lo = slots & (LANES - 1)
    at = iota((geo.wells, LANES), 1)
    piece = lax.div(at, geo.cap)
    position = (lax.rem(at, geo.cap) + 1).astype(F32)
    found = jnp.zeros((2 * geo.wells, LANES), F32)
    for g in range(geo.groups):
        well = spread(slot_hi[g : g + 1], (geo.wells, LANES)) == iota((geo.wells, LANES), 0)
        device = (piece * geo.groups + (g + 1)).astype(F32)
        marks = jnp.concatenate([jnp.where(well, device, 0.0), jnp.where(well, position, 0.0)], axis=0)
        hot = one_hot(slot_lo[g : g + 1], LANES)
        found += lax.dot_general(marks.astype(BF16), hot, (((1,), (1,)), ((), ())), preferred_element_type=F32)
    inv_dev[...] = found[: geo.wells].astype(jnp.int32) - 1
    inv_pos[...] = jnp.maximum(found[geo.wells :].astype(jnp.int32) - 1, 0)


def relay(geo, came, back):
    shape = (geo.devices, LANES)
    at = iota(shape, 0)
    even = (iota(shape, 1) & 1) == 0
    within = lax.rem(at, geo.n_gy)
    faces = jnp.full(shape, lax.axis_index(AXES), jnp.int32) < geo.faces
    up, down, count = geo.n_gy, geo.devices - geo.n_gy, geo.devices
    one, two = came.get(1), came.get(2)
    after = jnp.where(at < down, pltpu.roll(one, down, 0), 0.0)
    before = jnp.where(at >= up, pltpu.roll(two, up, 0), 0.0)

    def beside(block):
        low = jnp.where(within > 0, pltpu.roll(pltpu.roll(block, 1, 1), 1, 0), 0.0)
        high = jnp.where(within < geo.n_gy - 1, pltpu.roll(pltpu.roll(block, LANES - 1, 1), count - 1, 0), 0.0)
        return jnp.where(even, high, low)

    back.put(1, jnp.where(faces, after, beside(one)))
    back.put(2, jnp.where(faces, before, beside(two)))


def at_segments(geo, came, inv_dev, inv_pos, offset):
    shape = (geo.wells, LANES)
    device = inv_dev[...]
    position = inv_pos[...] + offset
    kept = [jnp.zeros(shape, F32) for _ in range(4)]
    for s in range(geo.devices):
        found = take_lanes(spread(came.get(0, s, 1), shape), position)
        kept[s % 4] = jnp.where(device == s, found, kept[s % 4])
    return (kept[0] + kept[1]) + (kept[2] + kept[3])


def at_slots(geo, rows, hi, lo):
    shape = (geo.devices, LANES)
    kept = jnp.zeros(shape, F32)
    for w in range(geo.wells):
        found = take_lanes(spread(rows[w], shape), lo)
        kept = jnp.where(hi == w, found, kept)
    return kept


def solve_segments(geo, rate, inverse):
    shape = (geo.segs, LANES)
    own = iota(shape, 0) == iota(shape, 1)
    rows = []
    for w in range(geo.wells):
        sums = jnp.sum(inverse[w] * rate[w : w + 1, :], axis=1, keepdims=True)
        rows.append(jnp.sum(jnp.where(own, spread(sums, shape), 0.0), axis=0, keepdims=True))
    return rows


def owner_first_body(geo, came, inv_dev, inv_pos, hi_ref, lo_ref, inverse_held, well_in, well_out, back):
    came, back = Rows(came, 3), Rows(back, 5)
    hi, lo = hi_ref[...], lo_ref[...]
    rows_in = [[well_in[c : c + 1, w * LANES : (w + 1) * LANES] for w in range(geo.wells)] for c in range(3)]
    rows_out = [[well_out[c : c + 1, w * LANES : (w + 1) * LANES] for w in range(geo.wells)] for c in range(3)]
    rate = jnp.zeros((geo.wells, LANES), F32)
    for c in range(3):
        rate += jnp.concatenate(rows_in[c], axis=0) * at_segments(geo, came, inv_dev, inv_pos, c * geo.cap)
    back.put(0, at_slots(geo, solve_segments(geo, rate, inverse_held), hi, lo))
    relay(geo, came, back)
    for place, rows in ((3, rows_in), (4, rows_out)):
        block = jnp.zeros((geo.devices, LANES), F32)
        for c in range(3):
            part = at_slots(geo, rows[c], hi, lo)
            block += pltpu.roll(part, c * geo.cap, 1) if c else part
        back.put(place, block)


def owner_body(geo, came, inv_dev, inv_pos, hi_ref, lo_ref, inverse_held, back, sums):
    came, back = Rows(came, 3), Rows(back, 3)
    rate = at_segments(geo, came, inv_dev, inv_pos, 0)
    back.put(0, at_slots(geo, solve_segments(geo, rate, inverse_held), hi_ref[...], lo_ref[...]))
    relay(geo, came, back)
    sums[...] = spread(jnp.sum(came.get(0), axis=0, keepdims=True), sums.shape)


def scatter_terms(geo, came, coeff_out, rowp, spot_hot, packed, left, spots):
    pack_slots(geo, came, 0, 0, packed)
    rate = packed[...]
    parts = []
    for c in range(3):
        value = coeff_out[c] * rate
        high = value.astype(BF16)
        parts += [high, (value - high.astype(F32)).astype(BF16)]
    n = geo.half_rows
    row = rowp[...]
    row = jnp.where(row >= n, row - n, row)
    for g in range(geo.groups):
        hot = one_hot(row[g : g + 1], n)
        for i, part in enumerate(parts):
            left[i * n : (i + 1) * n, g * LANES : (g + 1) * LANES] = hot * spread(part[g : g + 1], hot.shape)
    result = lax.dot_general(left[...], spot_hot[...], (((1,), (1,)), ((), ())), preferred_element_type=F32)
    for c in range(3):
        i = 2 * c * n
        summed = result[i : i + n] + result[i + n : i + 2 * n]
        for h in range(2):
            low = c * geo.tile_rows + h * n
            spots[low : low + n, :] = summed[:, h * LANES : (h + 1) * LANES]


def apply_operator(geo, came, vector, flux, diag, face, spots, store):
    at_row, at_lane = iota((SUBS, LANES), 0), iota(geo.tile, 1)
    edges = jnp.concatenate([came.get(1, geo.faces, SUBS), came.get(2, geo.faces, SUBS)], axis=0)
    for z in range(geo.layers):
        f = [face[n, z].astype(F32) for n in range(6)]
        v = [vector[z, b] for b in range(3)]
        for a in range(3):
            j = 3 * z + a
            base = geo.base(j)
            block = flux[base : base + geo.rows, :]
            first = jnp.where(at_row == 0, spread(came.get(2, j, 1), at_row.shape), flux[base - 1 : base - 1 + SUBS, :])
            under = jnp.concatenate([first, flux[base - 1 + SUBS : base - 1 + geo.rows, :]], axis=0)
            final = jnp.where(at_row == SUBS - 1, spread(came.get(1, j, 1), at_row.shape), flux[base + 1 + SUBS : base + 1 + geo.rows, :])
            over = jnp.concatenate([flux[base + 1 : base + 1 + SUBS, :], final], axis=0)
            ends = pltpu.roll(edges, LANES - 1 - 2 * j, 1)
            left = jnp.where(at_lane == 0, ends, pltpu.roll(block, 1, 1))
            right = jnp.where(at_lane == LANES - 1, ends, pltpu.roll(block, LANES - 1, 1))
            beside = f[0] * under + f[1] * over + f[2] * left + f[3] * right
            if z > 0:
                beside += f[4] * flux[base - 3 * geo.rows : base - 2 * geo.rows, :]
            if z + 1 < geo.layers:
                beside += f[5] * flux[base + 3 * geo.rows : base + 4 * geo.rows, :]
            own = diag[z, a, 0].astype(F32) * v[0]
            own += diag[z, a, 1].astype(F32) * v[1]
            own += diag[z, a, 2].astype(F32) * v[2]
            low = a * geo.tile_rows + z * geo.rows
            store(z, a, own - beside - spots[low : low + geo.rows, :])


def send_next(geo, source, inverse, mobility, rowp, lanep, coeff_in, dots, ahead, flux, send, packed):
    def put(z, c, block):
        ahead[z, c] = block

    precondition(geo, inverse, lambda z, c: source[z, c], put)
    at = iota((1, LANES), 1)
    row = jnp.zeros((1, LANES), F32)
    for n, dot in enumerate(dots):
        row = jnp.where(at == geo.cap + n, spread(total(dot), (1, LANES)), row)
    send.put(0, spread(row, (geo.devices, LANES)))
    packed[...] = jnp.zeros_like(packed)

    def finish(g, kept):
        rate = kept[0] * spread(coeff_in[0, g : g + 1, :], kept[0].shape)
        rate += kept[1] * spread(coeff_in[1, g : g + 1, :], kept[0].shape)
        rate += kept[2] * spread(coeff_in[2, g : g + 1, :], kept[0].shape)
        packed[g : g + 1, :] = jnp.sum(rate, axis=0, keepdims=True)

    gather_cells(geo, ahead, rowp, lanep, finish)
    write_flux(geo, mobility, ahead, flux)
    write_faces(geo, flux, send)
    unpack_slots(geo, packed[...], 0, send)


def stage_body(geo, rule, n_in, n_out, goes_on, *refs):
    refs = list(refs)

    def take(n):
        got, refs[:n] = refs[:n], []
        return got

    came, vector, flux_in, rowp, lanep, spot_hot = take(6)
    inputs = take(n_in)
    diag, face, *hats = take(4 if goes_on else 2)
    outputs = take(n_out)
    following = take(3) if goes_on else take(1)
    packed, left, spots = take(3)
    came = Rows(came, came.shape[0] // geo.devices)
    coeff_in, coeff_out, store, source, dots = rule(came, packed, inputs, outputs)
    scatter_terms(geo, came, coeff_out, rowp, spot_hot, packed, left, spots)
    apply_operator(geo, came, vector, flux_in, diag, face, spots, store)
    if goes_on:
        ahead, flux, send = following
        send = Rows(send, 3)
        send_next(geo, source, *hats, rowp, lanep, coeff_in, dots, ahead, flux, send, packed)
    else:
        at = iota((1, LANES), 1)
        row = jnp.where(at == 0, spread(total(dots[0]), (1, LANES)), spread(total(dots[1]), (1, LANES)))
        following[0][...] = spread(row, following[0].shape)


def zeros(geo, count):
    return [jnp.zeros(geo.tile, F32) for _ in range(count)]


def pick(sums, geo, n):
    return sums[0:1, geo.cap + n : geo.cap + n + 1]


def keep(ref, value):
    ref[...] = spread(value, ref.shape)


def residual_rule(geo, came, packed, inputs, outputs):
    (right_side,) = inputs
    shadow, coeff_in, coeff_out = outputs
    for c in range(3):
        pack_slots(geo, came, 3, c * geo.cap, packed)
        coeff_in[c] = packed[...]
        pack_slots(geo, came, 4, c * geo.cap, packed)
        coeff_out[c] = packed[...]
    dots = zeros(geo, 1)

    def store(z, c, image):
        value = right_side[z, c] - image
        shadow[z, c] = value
        dots[0] += value * value

    return coeff_in, coeff_out, store, shadow, dots


def image_rule(geo, came, packed, inputs, outputs):
    coeff_in, coeff_out, shadow = inputs
    (applied,) = outputs
    dots = zeros(geo, 1)

    def store(z, c, image):
        applied[z, c] = image
        dots[0] += shadow[z, c] * image

    return coeff_in, coeff_out, store, applied, dots


def half_rule(geo, came, packed, inputs, outputs):
    coeff_in, coeff_out, shadow, rho_sums, rho_at, sums, residual, applied, behind = inputs
    step_out, deeper, half, response = outputs
    step = rho_sums[0:1, rho_at : rho_at + 1] / pick(sums, geo, 0)
    keep(step_out, step)
    step = spread(step, geo.tile)
    dots = zeros(geo, 4)

    def store(z, c, image):
        deeper[z, c] = image
        s = residual[z, c] - step * applied[z, c]
        t = behind[z, c] - step * image
        half[z, c] = s
        response[z, c] = t
        dots[0] += t * s
        dots[1] += t * t
        dots[2] += shadow[z, c] * t
        dots[3] += shadow[z, c] * s

    return coeff_in, coeff_out, store, response, dots


def next_rule(geo, came, packed, inputs, outputs):
    coeff_in, coeff_out, shadow, rho_sums, rho_at, step_in, sums, half, response, applied, deeper, search, moved = inputs
    rho_out, residual_next, behind_next, applied_next, search_next, moved_next = outputs
    smoothing = pick(sums, geo, 0) / pick(sums, geo, 1)
    rho_next = pick(sums, geo, 3) - smoothing * pick(sums, geo, 2)
    step = step_in[0:1, 0:1]
    momentum = (rho_next / rho_sums[0:1, rho_at : rho_at + 1]) * (step / smoothing)
    keep(rho_out, rho_next)
    smoothing, momentum, step = (spread(x, geo.tile) for x in (smoothing, momentum, step))
    dots = zeros(geo, 1)

    def store(z, c, image):
        t = response[z, c]
        s = half[z, c]
        p = search[z, c]
        v = applied[z, c]
        r = s - smoothing * t
        w = t - smoothing * image
        v_next = w + momentum * (v - smoothing * deeper[z, c])
        residual_next[z, c] = r
        behind_next[z, c] = w
        applied_next[z, c] = v_next
        search_next[z, c] = r + momentum * (p - smoothing * v)
        by = step * p + smoothing * s
        moved_next[z, c] = by if moved is None else moved[z, c] + by
        dots[0] += shadow[z, c] * v_next

    return coeff_in, coeff_out, store, applied_next, dots


def last_rule(geo, came, packed, inputs, outputs):
    coeff_out, rho_sums, rho_at, sums, residual, applied, behind, search, moved = inputs
    half, response, moved_next = outputs
    step = spread(rho_sums[0:1, rho_at : rho_at + 1] / pick(sums, geo, 0), geo.tile)
    dots = zeros(geo, 2)

    def store(z, c, image):
        s = residual[z, c] - step * applied[z, c]
        t = behind[z, c] - step * image
        half[z, c] = s
        response[z, c] = t
        by = step * search[z, c]
        moved_next[z, c] = by if moved is None else moved[z, c] + by
        dots[0] += t * s
        dots[1] += t * t

    return None, coeff_out, store, None, dots


def finish_body(geo, came, moved, half, response, guess, inverse, solution_out, residual_out, solution, residual, sems):
    sums = jnp.sum(came[...], axis=0, keepdims=True)
    smoothing = spread(sums[:, 0:1] / sums[:, 1:2], geo.tile)
    copies = []

    def leave(source, target, layer, sem):
        copies.append(pltpu.make_async_copy(source.at[layer], target.at[layer], sem))
        copies[-1].start()

    for z, c in geo.tiles():
        residual[z, c] = half[z, c] - smoothing * response[z, c]
    copies.append(pltpu.make_async_copy(residual, residual_out, sems.at[0, 0]))
    copies[-1].start()

    def put(z, c, block):
        solution[z, c] = guess[z, c] + block
        if z % 2 and c + 1 == geo.comps:
            leave(solution, solution_out, z - 1, sems.at[1, z - 1])
            leave(solution, solution_out, z, sems.at[1, z])

    precondition(geo, inverse, lambda z, c: moved[z, c] + smoothing * half[z, c], put)
    for copy in copies:
        copy.wait()


def exchange(geo, rows):
    wide = rows.reshape(geo.devices, 1, rows.size // geo.devices)
    return lax.all_to_all(wide, AXES, split_axis=0, concat_axis=0, tiled=True).reshape(rows.shape)


def per_device(right_side, guess, diag, mobility, face, inverse, perf_cell, perf_slot, well_in, well_out, well_inverse):
    geo = Geometry(right_side.shape, perf_cell.shape[1:], well_inverse.shape, lax.axis_size("gy"))
    ints = jnp.int32
    block = (geo.devices, LANES)
    packed = (geo.groups_pad, LANES)
    seg = (geo.wells, LANES)
    wide = ((3 * geo.devices, LANES), F32)
    small = ((SUBS, LANES), F32)
    vec = (geo.vector, F32)
    coeffs = ((3,) + packed, F32)
    sent = [vec, (geo.flux, F32), wide]

    table = (perf_cell.shape[1:], ints)
    flux, send, rowp, lanep, spot_hot, hi, lo, inv_dev, inv_pos, inverse_held, guess_held, mobility, well_in, well_out = call(
        functools.partial(first_body, geo),
        [(geo.flux, F32), wide, (packed, ints), (packed, ints), ((2 * LANES, geo.slots), BF16), (block, ints), (block, ints),
         (seg, ints), (seg, ints), (well_inverse.shape, F32), vec, (mobility.shape, BF16), (well_in.shape, F32), (well_out.shape, F32)],
        [], far=[perf_cell[0], perf_slot[0], guess, mobility, well_inverse, well_in, well_out],
        scratch=[pltpu.VMEM(*table), pltpu.VMEM(*table), pltpu.VMEM(block, ints),
                 pltpu.VMEM(packed, ints), pltpu.VMEM((3,) + packed, F32), pltpu.SemaphoreType.DMA((7,))],
    )
    owner_tables = [inv_dev, inv_pos, hi, lo, inverse_held]
    scratch = [pltpu.VMEM(packed, F32), pltpu.VMEM((6 * geo.half_rows, geo.slots), BF16), pltpu.VMEM((3 * geo.tile_rows, LANES), F32)]

    def stage(rule, outs, came, vector, flux, inputs, goes_on=True):
        arrays = [i for i in inputs if i is not None and not isinstance(i, int)]

        def placed(came, packed, refs, out_refs):
            rest = list(refs)
            return rule(geo, came, packed, [i if i is None or isinstance(i, int) else rest.pop(0) for i in inputs], out_refs)

        return call(
            functools.partial(stage_body, geo, placed, len(arrays), len(outs), goes_on),
            outs + (sent if goes_on else [(block, F32)]),
            [came, vector, flux, rowp, lanep, spot_hot] + arrays + [diag, face] + ([inverse, mobility] if goes_on else []), scratch=scratch,
        )

    def owner(send):
        back, sums = call(functools.partial(owner_body, geo), [wide, small], [exchange(geo, send)] + owner_tables)
        return exchange(geo, back), sums

    (back,) = call(
        functools.partial(owner_first_body, geo), [((5 * geo.devices, LANES), F32)], [exchange(geo, send)] + owner_tables + [well_in, well_out]
    )
    shadow, coeff_in, coeff_out, ahead, flux, send = stage(residual_rule, [vec, coeffs, coeffs], exchange(geo, back), guess_held, flux, [right_side])
    always = [coeff_in, coeff_out, shadow]
    came, sums = owner(send)
    rho, rho_at = sums, geo.cap
    applied, ahead, flux, send = stage(image_rule, [vec], came, ahead, flux, always)
    residual, search, behind, moved = shadow, shadow, applied, None
    for iteration in range(ITERS):
        came, sums = owner(send)
        if iteration + 1 == ITERS:
            half, response, moved, send = stage(
                last_rule, [vec] * 3, came, ahead, flux,
                [coeff_out, rho, rho_at, sums, residual, applied, behind, search, moved], goes_on=False,
            )
            break
        step, deeper, half, response, ahead, flux, send = stage(
            half_rule, [small] + [vec] * 3, came, ahead, flux, always + [rho, rho_at, sums, residual, applied, behind]
        )
        came, sums = owner(send)
        rho, residual, behind, applied, search, moved, ahead, flux, send = stage(
            next_rule, [small] + [vec] * 5, came, ahead, flux,
            always + [rho, rho_at, step, sums, half, response, applied, deeper, search, moved],
        )
        rho_at = 0
    return call(
        functools.partial(finish_body, geo), [vec] * 2, [exchange(geo, send), moved, half, response, guess, inverse],
        scratch=[pltpu.VMEM(*vec), pltpu.VMEM(*vec), pltpu.SemaphoreType.DMA((2, geo.layers))], out_far=True,
    )


def solution(mesh):
    in_specs = (
        P(None, None, "gx", "gy"),
        P(None, None, "gx", "gy"),
        P(None, None, None, "gx", "gy"),
        P(None, None, None, "gx", "gy"),
        P(None, None, "gx", "gy"),
        P(None, None, None, "gx", "gy"),
        P(AXES, None, None),
        P(AXES, None, None),
        P(None, AXES),
        P(None, AXES),
        P(AXES, None, None),
    )
    out_specs = (P(None, None, "gx", "gy"), P(None, None, "gx", "gy"))
    return jax.shard_map(per_device, mesh=mesh, in_specs=in_specs, out_specs=out_specs, check_vma=False)
```
